32 devices in a mesh: grp: 8 (over y, x, core), blk: 4 (over z).
Axes of the slice: x: 2, y: 2, z: 4, core: 2. Of those that a mesh axis runs over, the one named last changes fastest.
Arguments:
- embed: bfloat16 [16384, 1024], P(('grp', 'blk')), may hold values from -6 to 6
- dest: int32 [16384], P(('grp', 'blk')), may hold values from 0 to 31, as said below
- slot: int32 [16384], P(('grp', 'blk')), may hold values from 0 to 511, as said below
Outputs:
- best: float32 [16384], P(('grp', 'blk'))
The draws below stay inside these ranges and needn't reach their ends.
Inputs may be any that keep to these rules, and one draw needn't show every extreme that they name: Each device index receives exactly 512 documents; at most 32 documents of one device's rows name the same dest, and in every draw some device sends exactly 32 to some dest. The pairs (dest, slot) are all different.
All inputs are finite; a program needn't handle non-finite values.
Results may differ from the reference program's by a relative error of at most 0.0013.
Values may be sent and summed in bfloat16 or wider, within the bound.
No kernel may reach another device: no remote copies, remote signals or barrier semaphores. Data moves between devices by JAX's collectives and lax.ppermute only.
A program may use at most 64 MiB of HBM per device.

```python
import jax
import jax.numpy as jnp
from jax import lax

D = 1024
MEM_DEV = 512
DOCS = 16384
CLUSTER = 2048
N_GRP = 8
N_BLK = 4


def route_plan(key):
    ndev = N_GRP * N_BLK
    base = MEM_DEV // ndev
    half = base // 2
    steps = jnp.arange(ndev, dtype=jnp.int32)
    values = jnp.where(steps % 2 == 0, base - half, base + half).astype(jnp.int32)
    values = values.at[1].set(base + 2 * half).at[3].set(base)
    values = jax.random.permutation(jax.random.fold_in(key, 11), values)
    counts = values[(steps[None, :] - steps[:, None]) % ndev]
    row_start = jnp.cumsum(counts, axis=1) - counts
    row_end = row_start + counts
    col_start = jnp.cumsum(counts, axis=0) - counts
    src_keys = jax.random.split(jax.random.fold_in(key, 12), ndev)
    order = jax.vmap(lambda kk: jax.random.permutation(kk, MEM_DEV))(src_keys).astype(jnp.int32)
    target = jnp.sum((row_end[:, None, :] <= order[:, :, None]).astype(jnp.int32), axis=2)
    rank = order - jnp.take_along_axis(row_start, target, axis=1)
    arrival = jnp.take_along_axis(col_start, target, axis=1) + rank
    dst_keys = jax.random.split(jax.random.fold_in(key, 13), ndev)
    seats = jax.vmap(lambda kk: jax.random.permutation(kk, MEM_DEV))(dst_keys).astype(jnp.int32)
    slots = seats[target, arrival]
    return (target.reshape(-1).astype(jnp.int32), slots.reshape(-1).astype(jnp.int32))


def draw_dest(key, part):
    return route_plan(key)[0]


def draw_slot(key, part):
    return route_plan(key)[1]


def block_levels(rng, extent, cuts, least, largest):
    level = 1.0
    for axis_at, shards_of in cuts:
        steps = jax.random.uniform(jax.random.fold_in(jax.random.fold_in(rng, 6), axis_at), (shards_of,), jnp.float32, least / len(cuts), largest / len(cuts))
        level = level * jnp.repeat(jnp.exp(steps), extent[axis_at] // shards_of).reshape((-1,) + (1,) * (len(extent) - 1 - axis_at))
    return level


def scatter_about(own_key, extent, spread, reach, pieces=(), held_as=jnp.bfloat16):
    loudness = block_levels(own_key, extent, pieces, -0.22, 0.18) if pieces else 1.0
    entries = jax.random.normal(own_key, extent, jnp.float32) * spread * loudness
    return jnp.minimum(jnp.maximum(entries, -reach), reach).astype(held_as)


def setup_inputs(seed: int = 0) -> dict:
    keys = jax.random.split(jax.random.key(seed), 4)
    embed = scatter_about(keys[0], (DOCS, D), 1.0, 6.0, ((0, 32),))
    dest = draw_dest(jax.random.fold_in(keys[3], 71), 0)
    slot = draw_slot(jax.random.fold_in(keys[3], 71), 0)
    return {"embed": embed, "dest": dest, "slot": slot}


def reference(embed, dest, slot):
    position = dest * MEM_DEV + slot
    members = jnp.zeros((DOCS, D), jnp.bfloat16).at[position].set(embed)
    wide = members.astype(jnp.float32)
    unit = (wide * lax.rsqrt(lax.optimization_barrier(jnp.sum(wide * wide, axis=1, keepdims=True)) + 1e-06)).astype(jnp.bfloat16)
    groups = unit.reshape(N_GRP, CLUSTER, D)

    def per_group(group_unit):
        blocks = group_unit.reshape(N_BLK, MEM_DEV, D)

        def per_block(inputs):
            block, index = inputs
            scores = lax.dot_general(block, group_unit, (((1,), (1,)), ((), ())), preferred_element_type=jnp.float32)
            rows = index * MEM_DEV + jnp.arange(MEM_DEV, dtype=jnp.int32)
            cols = jnp.arange(CLUSTER, dtype=jnp.int32)
            scores = jnp.where(rows[:, None] == cols[None, :], jnp.float32(-3.0), scores)
            return lax.optimization_barrier(jnp.max(scores, axis=1))
        return lax.map(per_block, (blocks, jnp.arange(N_BLK, dtype=jnp.int32))).reshape(-1)
    best_member = lax.map(per_group, groups).reshape(-1)
    return best_member[position]
```

```python
import functools

import jax
import jax.numpy as jnp
from jax import lax
from jax.experimental import pallas as pl
from jax.experimental.pallas import tpu as pltpu
from jax.sharding import PartitionSpec as P


AXES = ("grp", "blk")
PAD = 2.0
LOW = -8.0
F32 = jnp.float32
BF16 = jnp.bfloat16
VMEM = pl.BlockSpec(memory_space=pltpu.VMEM)
SMEM = pl.BlockSpec(memory_space=pltpu.SMEM)
TILE = 256


def pack_kernel(nsec, cap, nblk, me_ref, dest_ref, embed_ref, *outs):
    pos_ref, sections = outs[0], outs[1:]
    count = embed_ref.shape[0]
    part = lax.div(dest_ref[...], nblk) ^ me_ref[0]
    onehot = lax.broadcasted_iota(jnp.int32, (nsec, count), 0) == part
    lower = lax.broadcasted_iota(jnp.int32, (count, count), 0) < lax.broadcasted_iota(
        jnp.int32, (count, count), 1
    )
    before = jnp.dot(
        onehot.astype(F32).astype(BF16), lower.astype(F32).astype(BF16), preferred_element_type=F32
    )
    rank = jnp.sum(jnp.where(onehot, before, 0.0), axis=0, keepdims=True).astype(jnp.int32)
    pos = part * cap + rank
    pos_ref[...] = pos
    wide = embed_ref[...].astype(F32)
    unit = (wide * lax.rsqrt(jnp.sum(wide * wide, axis=1, keepdims=True) + 1e-06)).astype(BF16)
    held = jnp.sum(onehot.astype(F32), axis=1, keepdims=True)
    rows = lax.broadcasted_iota(jnp.int32, (cap, 128), 0).astype(F32)
    first = lax.broadcasted_iota(jnp.int32, (cap, 128), 1) == 0
    for k, out in enumerate(sections):
        pick = lax.broadcasted_iota(jnp.int32, (cap, count), 0) + k * cap == pos
        out[...] = jnp.dot(
            pick.astype(F32).astype(BF16), unit, preferred_element_type=F32
        ).astype(BF16)
        mark = jnp.where(first & (rows >= held[k : k + 1, :]), PAD, 0.0)
        out[:, 0:128] = (out[:, 0:128].astype(F32) + mark).astype(BF16)


def pack(embed, dest, me, nsec, cap, nblk):
    count, width = embed.shape
    return pl.pallas_call(
        functools.partial(pack_kernel, nsec, cap, nblk),
        out_shape=[jax.ShapeDtypeStruct((1, count), jnp.int32)]
        + [jax.ShapeDtypeStruct((cap, width), BF16)] * nsec,
        in_specs=[SMEM, VMEM, VMEM],
        out_specs=[VMEM] * (nsec + 1),
        compiler_params=pltpu.CompilerParams(vmem_limit_bytes=24 << 20),
        name="pack",
    )(me, dest.reshape(1, count), embed)


def scores(left, right):
    return lax.dot_general(left, right, (((1,), (1,)), ((), ())), preferred_element_type=F32)


def pair_kernel(nold, owner_ref, new_ref, *refs):
    olds, bias_olds, best_olds = refs[:nold], refs[nold : 2 * nold], refs[2 * nold : 3 * nold]
    bias_ref, best_ref = refs[3 * nold], refs[3 * nold + 1]
    best_outs = refs[3 * nold + 2 : 4 * nold + 2]
    acc_ref = refs[4 * nold + 2]
    rows = new_ref.shape[0]

    @pl.when(owner_ref[0] == 1)
    def _():
        width = new_ref.shape[1]
        first = (lax.broadcasted_iota(jnp.int32, (8, width), 1) == 0).astype(F32).astype(BF16)
        bias_ref[...] = jnp.where(scores(first, new_ref[...])[0:1, :] > 1.0, LOW, 0.0)
        down = jnp.where(new_ref[:, 0:1].astype(F32) > 1.0, LOW, 0.0)
        acc_ref[...] = jnp.full_like(acc_ref, LOW)

        def fold(start, value):
            part = value[:, 0:128]
            for j in range(1, TILE // 128):
                part = jnp.maximum(part, value[:, j * 128 : (j + 1) * 128])
            acc_ref[start:, :] = jnp.maximum(acc_ref[start:, :], part)

        col_best = []
        for j in range(rows // TILE):
            lo = j * TILE
            value = scores(new_ref[lo:, :], new_ref[lo : lo + TILE, :])
            same = lax.broadcasted_iota(jnp.int32, value.shape, 0) == lax.broadcasted_iota(
                jnp.int32, value.shape, 1
            )
            value = jnp.where(same, LOW, value)
            fold(lo, value + bias_ref[:, lo : lo + TILE])
            col_best.append(jnp.max(value + down[lo:, :], axis=0, keepdims=True))
        for old, bias, best, out in zip(olds, bias_olds, best_olds, best_outs):

            def step(i, carry, old=old, bias=bias, best=best, out=out):
                at = pl.ds(pl.multiple_of(i * TILE, TILE), TILE)
                value = scores(new_ref[...], old[at, :])
                fold(0, value + bias[:, at])
                out[:, at] = jnp.maximum(
                    best[:, at], jnp.max(value + down, axis=0, keepdims=True)
                )
                return carry

            lax.fori_loop(0, old.shape[0] // TILE, step, 0)
        for j in range(rows // TILE):
            lo = j * TILE
            across = jnp.max(acc_ref[lo : lo + TILE, :].T, axis=0, keepdims=True)
            best_ref[:, lo : lo + TILE] = jnp.maximum(across, col_best[j])


def pair(owner, new, olds, biases, bests):
    rows, width = new.shape
    nold = len(olds)
    row = jax.ShapeDtypeStruct((1, rows), F32)
    flops = 2 * width * rows * (rows // 2 + sum(o.shape[0] for o in olds))
    out = pl.pallas_call(
        functools.partial(pair_kernel, nold),
        out_shape=[row, row] + [jax.ShapeDtypeStruct(b.shape, F32) for b in bests],
        in_specs=[SMEM] + [VMEM] * (1 + 3 * nold),
        out_specs=[VMEM] * (2 + nold),
        scratch_shapes=[pltpu.VMEM((rows, 128), F32)],
        compiler_params=pltpu.CompilerParams(vmem_limit_bytes=24 << 20),
        cost_estimate=pl.CostEstimate(flops=flops, bytes_accessed=rows * width * 2, transcendentals=0),
        name="pair",
    )(owner, new, *olds, *biases, *bests)
    return out[0], out[1], out[2:]


def pick_kernel(nsec, cap, pos_ref, got_ref, out_ref):
    count = pos_ref.shape[1]
    turned = got_ref[...].T
    total = jnp.zeros((1, count), F32)
    for k in range(nsec):
        hit = lax.broadcasted_iota(jnp.int32, (cap, count), 0) + k * cap == pos_ref[...]
        total = total + jnp.sum(jnp.where(hit, turned[:, k : k + 1], 0.0), axis=0, keepdims=True)
    out_ref[...] = total


def pick(pos, got, nsec, cap):
    return pl.pallas_call(
        functools.partial(pick_kernel, nsec, cap),
        out_shape=jax.ShapeDtypeStruct(pos.shape, F32),
        in_specs=[VMEM, VMEM],
        out_specs=VMEM,
        compiler_params=pltpu.CompilerParams(vmem_limit_bytes=8 << 20),
        name="pick",
    )(pos, got)


def on_device(embed, dest, slot):
    count, width = embed.shape
    nsec, nblk = lax.axis_size("grp"), lax.axis_size("blk")
    cap = 2 * count // (nsec * nblk) * nblk
    grp, blk = lax.axis_index("grp"), lax.axis_index("blk")
    upper = nblk // 2
    owner = (blk == upper - grp % 2).astype(jnp.int32).reshape(1)
    order = sorted((z for z in range(nblk) if z != upper), key=lambda z: abs(z - upper))

    def to_owner(z):
        flip = lambda b, core: b if core == 0 else nblk - 1 - b
        return [(g * nblk + flip(z, g % 2), g * nblk + flip(upper, g % 2)) for g in range(nsec)]

    pos, *sent = pack(embed, dest, grp.astype(jnp.int32).reshape(1), nsec, cap, nblk)
    xor = lambda k: [(g, g ^ k) for g in range(nsec)]
    held = [sent[0]] + [lax.ppermute(sent[k], "grp", xor(k)) for k in range(1, nsec)]
    per = max(1, TILE // cap)
    groups = [jnp.concatenate(held[q : q + per], axis=0) for q in range(0, nsec, per)]
    arrays, biases, bests = [], [], []

    def add(new):
        nonlocal bests
        bias, best, bests_now = pair(owner, new, arrays, biases, bests)
        arrays.append(new)
        biases.append(bias)
        bests = list(bests_now) + [best]

    for q, group in enumerate(groups):
        blocks = [group] + [lax.ppermute(group, AXES, to_owner(z)) for z in order]
        if q < len(groups) - 1:
            add(jnp.concatenate(blocks, axis=0))
        else:
            add(jnp.concatenate(blocks[:-1], axis=0))
            add(blocks[-1])
    size = per * cap
    last = jnp.concatenate(bests[-2:], axis=1)
    whole = jnp.concatenate([b.reshape(1, nblk, size) for b in bests[:-2] + [last]], axis=0)
    whole = jnp.swapaxes(whole, 0, 1).reshape(nblk, nsec, cap)
    own = jnp.where(owner == 1, whole[0], 0.0)
    for j, z in enumerate(order):
        own = own + lax.ppermute(whole[j + 1], AXES, [(b, a) for a, b in to_owner(z)])
    bit = 1
    back = own
    while bit < nsec:
        view = back.reshape(nsec // (2 * bit), 2, bit, cap)
        other = lax.ppermute(view[:, 1], "grp", xor(bit))
        back = jnp.stack([view[:, 0], other], axis=1).reshape(nsec, cap)
        bit *= 2
    return pick(pos, back, nsec, cap).reshape(count)


def solution(mesh):
    placed = (P(AXES, None), P(AXES), P(AXES))
    return jax.shard_map(
        on_device, mesh=mesh, in_specs=placed, out_specs=P(AXES), check_vma=False
    )
```

```python
import functools

import jax
import jax.numpy as jnp
from jax import lax
from jax.experimental import pallas as pl
from jax.experimental.pallas import tpu as pltpu
from jax.sharding import PartitionSpec as P


AXES = ("grp", "blk")
PAD = 2.0
LOW = -8.0
FULL = 4.0
REDO = 100.0
F32 = jnp.float32
BF16 = jnp.bfloat16
VMEM = pl.BlockSpec(memory_space=pltpu.VMEM)
SMEM = pl.BlockSpec(memory_space=pltpu.SMEM)
TILE = 256


def pack_kernel(nsec, cap, nblk, me_ref, dest_ref, embed_ref, *outs):
    pos_ref, sections = outs[0], outs[1:]
    count = embed_ref.shape[0]
    part = lax.div(dest_ref[...], nblk) ^ me_ref[0]
    onehot = lax.broadcasted_iota(jnp.int32, (nsec, count), 0) == part
    lower = lax.broadcasted_iota(jnp.int32, (count, count), 0) < lax.broadcasted_iota(
        jnp.int32, (count, count), 1
    )
    before = jnp.dot(
        onehot.astype(F32).astype(BF16), lower.astype(F32).astype(BF16), preferred_element_type=F32
    )
    rank = jnp.sum(jnp.where(onehot, before, 0.0), axis=0, keepdims=True).astype(jnp.int32)
    pos = part * cap + rank
    pos_ref[...] = pos
    wide = embed_ref[...].astype(F32)
    unit = (wide * lax.rsqrt(jnp.sum(wide * wide, axis=1, keepdims=True) + 1e-06)).astype(BF16)
    held = jnp.sum(onehot.astype(F32), axis=1, keepdims=True)
    rows = lax.broadcasted_iota(jnp.int32, (cap, 128), 0).astype(F32)
    first = lax.broadcasted_iota(jnp.int32, (cap, 128), 1) == 0
    for k, out in enumerate(sections):
        pick = lax.broadcasted_iota(jnp.int32, (cap, count), 0) + k * cap == pos
        out[...] = jnp.dot(
            pick.astype(F32).astype(BF16), unit, preferred_element_type=F32
        ).astype(BF16)
        mark = jnp.where(first & (rows >= held[k : k + 1, :]), PAD, 0.0)
        out[:, 0:128] = (out[:, 0:128].astype(F32) + mark).astype(BF16)


def pack(embed, dest, me, nsec, cap, nblk):
    count, width = embed.shape
    return pl.pallas_call(
        functools.partial(pack_kernel, nsec, cap, nblk),
        out_shape=[jax.ShapeDtypeStruct((1, count), jnp.int32)]
        + [jax.ShapeDtypeStruct((cap, width), BF16)] * nsec,
        in_specs=[SMEM, VMEM, VMEM],
        out_specs=[VMEM] * (nsec + 1),
        compiler_params=pltpu.CompilerParams(vmem_limit_bytes=24 << 20),
        name="pack",
    )(me, dest.reshape(1, count), embed)


def scores(left, right):
    return lax.dot_general(left, right, (((1,), (1,)), ((), ())), preferred_element_type=F32)


def first_entries(rows_ref):
    first = lax.broadcasted_iota(jnp.int32, (8, rows_ref.shape[1]), 1) == 0
    return scores(first.astype(F32).astype(BF16), rows_ref[...])[0:1, :]


def squeeze_kernel(nsec, *refs):
    sections, out_ref, pos_ref = refs[:nsec], refs[nsec], refs[nsec + 1]
    room = out_ref.shape[0]
    cap = sections[0].shape[0]
    size = nsec * cap
    filled = jnp.concatenate([first_entries(s) for s in sections], axis=1) < 1.5
    lower = lax.broadcasted_iota(jnp.int32, (size, size), 0) < lax.broadcasted_iota(
        jnp.int32, (size, size), 1
    )
    ones = jnp.broadcast_to(filled.astype(F32), (8, size))
    before = jnp.dot(
        ones.astype(BF16), lower.astype(F32).astype(BF16), preferred_element_type=F32
    )[0:1, :]
    total = jnp.sum(filled.astype(F32), axis=1, keepdims=True)
    pos = jnp.where(filled, before, -1.0).astype(jnp.int32)
    pos_ref[...] = pos
    pick = (lax.broadcasted_iota(jnp.int32, (room, size), 0) == pos).astype(F32).astype(BF16)
    value = jnp.dot(pick[:, 0:cap], sections[0][...], preferred_element_type=F32)
    for k in range(1, nsec):
        value = value + jnp.dot(
            pick[:, k * cap : (k + 1) * cap], sections[k][...], preferred_element_type=F32
        )
    out_ref[...] = value.astype(BF16)
    rows = lax.broadcasted_iota(jnp.int32, (room, 128), 0).astype(F32)
    first = lax.broadcasted_iota(jnp.int32, (room, 128), 1) == 0
    head = jnp.where(first & (rows >= total), PAD, value[:, 0:128])
    head = jnp.where(first & (rows == room - 1.0) & (total > room), FULL, head)
    out_ref[:, 0:128] = head.astype(BF16)


def squeeze(sections, room):
    cap, width = sections[0].shape
    size = len(sections) * cap
    return pl.pallas_call(
        functools.partial(squeeze_kernel, len(sections)),
        out_shape=[
            jax.ShapeDtypeStruct((room, width), BF16),
            jax.ShapeDtypeStruct((1, size), jnp.int32),
        ],
        in_specs=[VMEM] * len(sections),
        out_specs=[VMEM] * 2,
        compiler_params=pltpu.CompilerParams(vmem_limit_bytes=12 << 20),
        cost_estimate=pl.CostEstimate(
            flops=2 * room * size * width, bytes_accessed=2 * (room + size) * width, transcendentals=0
        ),
        name="squeeze",
    )(*sections)


def bias_of(entries):
    return jnp.where(entries > 3.0, REDO, jnp.where(entries > 1.5, LOW, 0.0))


def pair_kernel(nblk, nold, final, owner_ref, *refs):
    refs = list(refs)
    take = lambda n: [refs.pop(0) for _ in range(n)]
    blocks, olds, bias_olds, best_olds = take(nblk), take(nold), take(nold), take(nold)
    (new_ref, bias_ref, best_ref), best_outs = take(3), take(nold)
    rets = take(nblk if final else 0)
    (acc_ref,) = take(1)
    rows, size = new_ref.shape[0], blocks[0].shape[0]
    tile = TILE if rows % TILE == 0 else size

    @pl.when(owner_ref[0] == 1)
    def _():
        for j, block in enumerate(blocks):
            new_ref[j * size : (j + 1) * size, :] = block[...]
        bias_ref[...] = bias_of(first_entries(new_ref))
        down = bias_of(new_ref[:, 0:1].astype(F32))
        acc_ref[...] = jnp.full_like(acc_ref, LOW)

        def fold(start, value):
            part = value[:, 0:128]
            for j in range(1, value.shape[1] // 128):
                part = jnp.maximum(part, value[:, j * 128 : (j + 1) * 128])
            acc_ref[start:, :] = jnp.maximum(acc_ref[start:, :], part)

        col_best = []
        for j in range(rows // tile):
            lo = j * tile
            value = scores(new_ref[lo:, :], new_ref[lo : lo + tile, :])
            same = lax.broadcasted_iota(jnp.int32, value.shape, 0) == lax.broadcasted_iota(
                jnp.int32, value.shape, 1
            )
            value = jnp.where(same, LOW, value)
            fold(lo, value + bias_ref[:, lo : lo + tile])
            col_best.append(jnp.max(value + down[lo:, :], axis=0, keepdims=True))
        for old, bias, best, out in zip(olds, bias_olds, best_olds, best_outs):

            def step(i, carry, old=old, bias=bias, best=best, out=out):
                at = pl.ds(pl.multiple_of(i * tile, tile), tile)
                value = scores(new_ref[...], old[at, :])
                fold(0, value + bias[:, at])
                out[:, at] = jnp.maximum(
                    best[:, at], jnp.max(value + down, axis=0, keepdims=True)
                )
                return carry

            lax.fori_loop(0, old.shape[0] // tile, step, 0)
        for j in range(rows // tile):
            lo = j * tile
            across = jnp.max(acc_ref[lo : lo + tile, :].T, axis=0, keepdims=True)
            best_ref[:, lo : lo + tile] = jnp.maximum(across, col_best[j])
        for j, ret in enumerate(rets):
            ret[...] = jnp.full_like(ret, LOW)
            for q, best in enumerate(best_outs + [best_ref]):
                ret[q : q + 1, 0:size] = best[:, j * size : (j + 1) * size]


def ceil_to(n, m):
    return -(-n // m) * m


def pair(owner, blocks, olds, biases, bests, final):
    nblk, (size, width) = len(blocks), blocks[0].shape
    rows, nold = nblk * size, len(olds)
    row = jax.ShapeDtypeStruct((1, rows), F32)
    ret = jax.ShapeDtypeStruct((ceil_to(nold + 1, 8), ceil_to(size, 128)), F32)
    flops = 2 * width * rows * (rows // 2 + sum(o.shape[0] for o in olds))
    out = pl.pallas_call(
        functools.partial(pair_kernel, nblk, nold, final),
        out_shape=[jax.ShapeDtypeStruct((rows, width), BF16), row, row]
        + [row] * nold
        + [ret] * (nblk if final else 0),
        in_specs=[SMEM] + [VMEM] * (nblk + 3 * nold),
        out_specs=[VMEM] * (3 + nold + (nblk if final else 0)),
        scratch_shapes=[pltpu.VMEM((rows, 128), F32)],
        compiler_params=pltpu.CompilerParams(vmem_limit_bytes=24 << 20),
        cost_estimate=pl.CostEstimate(
            flops=flops, bytes_accessed=rows * width * 2, transcendentals=0
        ),
        name="pair",
    )(owner, *blocks, *olds, *biases, *bests)
    return out[0], out[1], list(out[3 : 3 + nold]) + [out[2]], out[3 + nold :]


def spread_kernel(nret, nq, per, owner_ref, *refs):
    rets, poss, out_ref = refs[:nret], refs[nret : nret + nq], refs[nret + nq]
    came = rets[1][...]
    for ret in rets[2:]:
        came = came + ret[...]
    value = jnp.where(owner_ref[0] == 1, rets[0][...], came)
    top = jnp.max(value)
    turned = value.T
    cap = out_ref.shape[1]
    for q, pos_ref in enumerate(poss):
        pos = pos_ref[...]
        hit = lax.broadcasted_iota(jnp.int32, (turned.shape[0], per * cap), 0) == pos
        back = jnp.max(jnp.where(hit, turned[:, q : q + 1], LOW), axis=0, keepdims=True)
        back = jnp.where(pos < 0, top, back)
        for i in range(per):
            k = q * per + i
            out_ref[k : k + 1, :] = back[:, i * cap : (i + 1) * cap]


def spread(owner, rets, poss, nsec, cap):
    return pl.pallas_call(
        functools.partial(spread_kernel, len(rets), len(poss), nsec // len(poss)),
        out_shape=jax.ShapeDtypeStruct((nsec, cap), F32),
        in_specs=[SMEM] + [VMEM] * (len(rets) + len(poss)),
        out_specs=VMEM,
        compiler_params=pltpu.CompilerParams(vmem_limit_bytes=8 << 20),
        name="spread",
    )(owner, *rets, *poss)


def pick_kernel(nsec, cap, pos_ref, got_ref, out_ref, redo_ref):
    count = pos_ref.shape[1]
    got = got_ref[...]
    redo_ref[0] = (jnp.max(got) > 0.5 * REDO).astype(jnp.int32)
    turned = got.T
    total = jnp.zeros((1, count), F32)
    for k in range(nsec):
        hit = lax.broadcasted_iota(jnp.int32, (cap, count), 0) + k * cap == pos_ref[...]
        total = total + jnp.sum(jnp.where(hit, turned[:, k : k + 1], 0.0), axis=0, keepdims=True)
    out_ref[...] = total


def pick(pos, got, nsec, cap):
    return pl.pallas_call(
        functools.partial(pick_kernel, nsec, cap),
        out_shape=[
            jax.ShapeDtypeStruct(pos.shape, F32),
            jax.ShapeDtypeStruct((1,), jnp.int32),
        ],
        in_specs=[VMEM, VMEM],
        out_specs=[VMEM, SMEM],
        compiler_params=pltpu.CompilerParams(vmem_limit_bytes=8 << 20),
        name="pick",
    )(pos, got)


def xor(nsec, bits):
    return [(g, g ^ bits) for g in range(nsec)]


def home(own, nsec):
    cap = own.shape[1]
    view = own.reshape(nsec // 2, 2, cap)
    swapped = lax.ppermute(view[:, 1], "grp", xor(nsec, 1))
    view = jnp.stack([view[:, 0], swapped], axis=1)
    parts = [view[0]] + [lax.ppermute(view[k], "grp", xor(nsec, 2 * k)) for k in range(1, nsec // 2)]
    return jnp.concatenate(parts, axis=0)


def best_of_all(held, owner, pos, room, per, nblk):
    nsec, cap = len(held), held[0].shape[0]
    upper = nblk // 2
    order = sorted((z for z in range(nblk) if z != upper), key=lambda z: abs(z - upper))
    flip = lambda b, core: b if core == 0 else nblk - 1 - b
    routes = [
        [(g * nblk + flip(z, g % 2), g * nblk + flip(upper, g % 2)) for g in range(nsec)]
        for z in order
    ]
    arrays, biases, bests, poss, rets = [], [], [], [], []
    groups = [squeeze(held[q : q + per], room) for q in range(0, nsec, per)]
    for q, (group, place) in enumerate(groups):
        poss.append(place)
        blocks = [group] + [lax.ppermute(group, AXES, route) for route in routes]
        new, bias, bests, rets = pair(owner, blocks, arrays, biases, bests, q == len(groups) - 1)
        arrays.append(new)
        biases.append(bias)
    came = [
        lax.ppermute(ret, AXES, [(b, a) for a, b in route]) for ret, route in zip(rets[1:], routes)
    ]
    own = spread(owner, [rets[0]] + came, poss, nsec, cap)
    return pick(pos, home(own, nsec), nsec, cap)


def on_device(embed, dest, slot):
    count = embed.shape[0]
    nsec, nblk = lax.axis_size("grp"), lax.axis_size("blk")
    cap = 2 * count // (nsec * nblk) * nblk
    grp, blk = lax.axis_index("grp"), lax.axis_index("blk")
    owner = (blk == nblk // 2 - grp % 2).astype(jnp.int32).reshape(1)
    pos, *sent = pack(embed, dest, grp.astype(jnp.int32).reshape(1), nsec, cap, nblk)
    held = [sent[0]] + [lax.ppermute(sent[k], "grp", xor(nsec, k)) for k in range(1, nsec)]
    per = max(1, TILE // cap)
    best, redo = best_of_all(held, owner, pos, 3 * per * cap // 4, per, nblk)
    best = lax.cond(
        redo[0] > 0,
        lambda: best_of_all(held, owner, pos, per * cap, per, nblk)[0],
        lambda: best,
    )
    return best.reshape(count)


def solution(mesh):
    placed = (P(AXES, None), P(AXES), P(AXES))
    return jax.shard_map(
        on_device, mesh=mesh, in_specs=placed, out_specs=P(AXES), check_vma=False
    )
```

```python
import functools

import jax
import jax.numpy as jnp
from jax import lax
from jax.experimental import pallas as pl
from jax.experimental.pallas import tpu as pltpu
from jax.sharding import PartitionSpec as P


AXES = ("grp", "blk")
PAD = 2.0
LOW = -8.0
FULL = 4.0
REDO = 100.0
F32 = jnp.float32
BF16 = jnp.bfloat16
VMEM = pl.BlockSpec(memory_space=pltpu.VMEM)
SMEM = pl.BlockSpec(memory_space=pltpu.SMEM)
TILE = 256


def pack_kernel(nsec, cap, nblk, me_ref, dest_ref, embed_ref, *outs):
    pos_ref, sections = outs[0], outs[1:]
    count = embed_ref.shape[0]
    cluster = lax.div(dest_ref[...], nblk)
    part = cluster ^ me_ref[0]
    onehot = lax.broadcasted_iota(jnp.int32, (nsec, count), 0) == part
    lower = lax.broadcasted_iota(jnp.int32, (count, count), 0) < lax.broadcasted_iota(
        jnp.int32, (count, count), 1
    )
    before = jnp.dot(
        onehot.astype(F32).astype(BF16), lower.astype(F32).astype(BF16), preferred_element_type=F32
    )
    rank = jnp.sum(jnp.where(onehot, before, 0.0), axis=0, keepdims=True).astype(jnp.int32)
    pos = part * cap + rank
    pos_ref[...] = cluster * cap + rank
    wide = embed_ref[...].astype(F32)
    unit = (wide * lax.rsqrt(jnp.sum(wide * wide, axis=1, keepdims=True) + 1e-06)).astype(BF16)
    held = jnp.sum(onehot.astype(F32), axis=1, keepdims=True)
    rows = lax.broadcasted_iota(jnp.int32, (cap, 128), 0).astype(F32)
    first = lax.broadcasted_iota(jnp.int32, (cap, 128), 1) == 0
    for k, out in enumerate(sections):
        pick = lax.broadcasted_iota(jnp.int32, (cap, count), 0) + k * cap == pos
        out[...] = jnp.dot(
            pick.astype(F32).astype(BF16), unit, preferred_element_type=F32
        ).astype(BF16)
        mark = jnp.where(first & (rows >= held[k : k + 1, :]), PAD, 0.0)
        out[:, 0:128] = (out[:, 0:128].astype(F32) + mark).astype(BF16)


def pack(embed, dest, me, nsec, cap, nblk):
    count, width = embed.shape
    return pl.pallas_call(
        functools.partial(pack_kernel, nsec, cap, nblk),
        out_shape=[jax.ShapeDtypeStruct((1, count), jnp.int32)]
        + [jax.ShapeDtypeStruct((cap, width), BF16)] * nsec,
        in_specs=[SMEM, VMEM, VMEM],
        out_specs=[VMEM] * (nsec + 1),
        compiler_params=pltpu.CompilerParams(vmem_limit_bytes=24 << 20),
        name="pack",
    )(me, dest.reshape(1, count), embed)


def scores(left, right):
    return lax.dot_general(left, right, (((1,), (1,)), ((), ())), preferred_element_type=F32)


def first_entries(rows_ref):
    first = lax.broadcasted_iota(jnp.int32, (8, rows_ref.shape[1]), 1) == 0
    return scores(first.astype(F32).astype(BF16), rows_ref[...])[0:1, :]


def squeeze_kernel(nsec, *refs):
    sections, out_ref, pos_ref = refs[:nsec], refs[nsec], refs[nsec + 1]
    room = out_ref.shape[0]
    cap = sections[0].shape[0]
    size = nsec * cap
    filled = jnp.concatenate([first_entries(s) for s in sections], axis=1) < 1.5
    lower = lax.broadcasted_iota(jnp.int32, (size, size), 0) < lax.broadcasted_iota(
        jnp.int32, (size, size), 1
    )
    ones = jnp.broadcast_to(filled.astype(F32), (8, size))
    before = jnp.dot(
        ones.astype(BF16), lower.astype(F32).astype(BF16), preferred_element_type=F32
    )[0:1, :]
    total = jnp.sum(filled.astype(F32), axis=1, keepdims=True)
    pos = jnp.where(filled, before, -1.0).astype(jnp.int32)
    pos_ref[...] = pos
    pick = (lax.broadcasted_iota(jnp.int32, (room, size), 0) == pos).astype(F32).astype(BF16)
    value = jnp.dot(pick[:, 0:cap], sections[0][...], preferred_element_type=F32)
    for k in range(1, nsec):
        value = value + jnp.dot(
            pick[:, k * cap : (k + 1) * cap], sections[k][...], preferred_element_type=F32
        )
    out_ref[...] = value.astype(BF16)
    rows = lax.broadcasted_iota(jnp.int32, (room, 128), 0).astype(F32)
    first = lax.broadcasted_iota(jnp.int32, (room, 128), 1) == 0
    head = jnp.where(first & (rows >= total), PAD, value[:, 0:128])
    head = jnp.where(first & (rows == room - 1.0) & (total > room), FULL, head)
    out_ref[:, 0:128] = head.astype(BF16)


def squeeze(sections, room):
    cap, width = sections[0].shape
    size = len(sections) * cap
    return pl.pallas_call(
        functools.partial(squeeze_kernel, len(sections)),
        out_shape=[
            jax.ShapeDtypeStruct((room, width), BF16),
            jax.ShapeDtypeStruct((1, size), jnp.int32),
        ],
        in_specs=[VMEM] * len(sections),
        out_specs=[VMEM] * 2,
        compiler_params=pltpu.CompilerParams(vmem_limit_bytes=12 << 20),
        cost_estimate=pl.CostEstimate(
            flops=2 * room * size * width, bytes_accessed=2 * (room + size) * width, transcendentals=0
        ),
        name="squeeze",
    )(*sections)


def bias_of(entries):
    return jnp.where(entries > 3.0, REDO, jnp.where(entries > 1.5, LOW, 0.0))


def pair_kernel(nblk, nold, unroll, owner_ref, *refs):
    refs = list(refs)
    take = lambda n: [refs.pop(0) for _ in range(n)]
    blocks, olds, bias_olds, best_olds = take(nblk), take(nold), take(nold), take(nold)
    (new_ref, bias_ref, best_ref), best_outs = take(3), take(nold)
    (acc_ref,) = take(1)
    rows, size = new_ref.shape[0], blocks[0].shape[0]
    tiles = lambda n: [(lo, min(TILE, n - lo)) for lo in range(0, n, TILE)]

    @pl.when(owner_ref[0] == 1)
    def _():
        for j, block in enumerate(blocks):
            new_ref[j * size : (j + 1) * size, :] = block[...]
        bias_ref[...] = bias_of(first_entries(new_ref))
        down = bias_of(new_ref[:, 0:1].astype(F32))
        acc_ref[...] = jnp.full_like(acc_ref, LOW)

        def fold(start, value):
            part = value[:, 0:128]
            for j in range(1, value.shape[1] // 128):
                part = jnp.maximum(part, value[:, j * 128 : (j + 1) * 128])
            acc_ref[start:, :] = jnp.maximum(acc_ref[start:, :], part)

        col_best = []
        for lo, tile in tiles(rows):
            value = scores(new_ref[lo:, :], new_ref[lo : lo + tile, :])
            same = lax.broadcasted_iota(jnp.int32, value.shape, 0) == lax.broadcasted_iota(
                jnp.int32, value.shape, 1
            )
            value = jnp.where(same, LOW, value)
            fold(lo, value + bias_ref[:, lo : lo + tile])
            col_best.append(jnp.max(value + down[lo:, :], axis=0, keepdims=True))
        for old, bias, best, out in zip(olds, bias_olds, best_olds, best_outs):

            def step(i, carry, old=old, bias=bias, best=best, out=out, tile=TILE):
                at = pl.ds(i * TILE, tile) if tile < TILE else pl.ds(pl.multiple_of(i * TILE, TILE), TILE)
                value = scores(new_ref[...], old[at, :])
                fold(0, value + bias[:, at])
                out[:, at] = jnp.maximum(
                    best[:, at], jnp.max(value + down, axis=0, keepdims=True)
                )
                return carry

            full, rest = divmod(old.shape[0], TILE)
            lax.fori_loop(0, full, step, 0, unroll=unroll if full % unroll == 0 else full)
            if rest:
                step(full, 0, tile=rest)
        for j, (lo, tile) in enumerate(tiles(rows)):
            across = jnp.max(acc_ref[lo : lo + tile, :].T, axis=0, keepdims=True)
            best_ref[:, lo : lo + tile] = jnp.maximum(across, col_best[j])


def ceil_to(n, m):
    return -(-n // m) * m


def pair(owner, blocks, olds, biases, bests, unroll):
    nblk, (size, width) = len(blocks), blocks[0].shape
    rows, nold = nblk * size, len(olds)
    row = jax.ShapeDtypeStruct((1, rows), F32)
    flops = 2 * width * rows * (rows // 2 + sum(o.shape[0] for o in olds))
    out = pl.pallas_call(
        functools.partial(pair_kernel, nblk, nold, unroll),
        out_shape=[jax.ShapeDtypeStruct((rows, width), BF16), row, row]
        + [jax.ShapeDtypeStruct(b.shape, F32) for b in bests],
        in_specs=[SMEM] + [VMEM] * (nblk + 3 * nold),
        out_specs=[VMEM] * (3 + nold),
        scratch_shapes=[pltpu.VMEM((rows, 128), F32)],
        compiler_params=pltpu.CompilerParams(vmem_limit_bytes=24 << 20),
        cost_estimate=pl.CostEstimate(
            flops=flops, bytes_accessed=rows * width * 2, transcendentals=0
        ),
        name="pair",
    )(owner, *blocks, *olds, *biases, *bests)
    return out[0], out[1], list(out[3:]) + [out[2]]


def every_kernel(nblk, owner_ref, *refs):
    blocks, best_ref, all_ref = refs[:nblk], refs[nblk], refs[nblk + 1]
    size = blocks[0].shape[0]
    count = nblk * size // TILE

    @pl.when(owner_ref[0] == 1)
    def _():
        for j, block in enumerate(blocks):
            all_ref[j * size : (j + 1) * size, :] = block[...]
        same = lax.broadcasted_iota(jnp.int32, (TILE, TILE), 0) == lax.broadcasted_iota(
            jnp.int32, (TILE, TILE), 1
        )
        span = lambda i: pl.ds(pl.multiple_of(i * TILE, TILE), TILE)

        def column(j, carry):
            def row(i, best):
                rows = all_ref[span(i), :]
                value = scores(rows, all_ref[span(j), :]) + bias_of(rows[:, 0:1].astype(F32))
                value = jnp.where(same & (i == j), LOW, value)
                return jnp.maximum(best, jnp.max(value, axis=0, keepdims=True))

            best_ref[:, span(j)] = lax.fori_loop(0, count, row, jnp.full((1, TILE), LOW, F32))
            return carry

        lax.fori_loop(0, count, column, 0)


def every(owner, blocks):
    nblk, (size, width) = len(blocks), blocks[0].shape
    return pl.pallas_call(
        functools.partial(every_kernel, nblk),
        out_shape=jax.ShapeDtypeStruct((1, nblk * size), F32),
        in_specs=[SMEM] + [VMEM] * nblk,
        out_specs=VMEM,
        scratch_shapes=[pltpu.VMEM((nblk * size, width), BF16)],
        compiler_params=pltpu.CompilerParams(vmem_limit_bytes=28 << 20),
        name="every",
    )(owner, *blocks)


def spread_kernel(nq, nblk, counts, zs, owner_ref, me_ref, *refs):
    bests, places, out_ref, rows_ref = refs[:nq], refs[nq : nq + nblk], refs[-2], refs[-1]
    cap = out_ref.shape[2]

    @pl.when(owner_ref[0] == 1)
    def _():
        me = me_ref[0]
        top = functools.reduce(jnp.maximum, [jnp.max(b[...]) for b in bests])
        k = 0
        for best, ns in zip(bests, counts):
            size = best.shape[1] // nblk
            for j in range(nblk):
                rows_ref[j : j + 1, 0:size] = best[:, j * size : (j + 1) * size]
            turned = rows_ref[...].T
            lo = k * cap
            for j, zz in enumerate(zs):
                pos = places[j][:, lo : lo + ns * cap]
                hit = lax.broadcasted_iota(jnp.int32, (size, ns * cap), 0) == pos
                back = jnp.max(
                    jnp.where(hit, turned[0:size, j : j + 1], LOW), axis=0, keepdims=True
                )
                back = jnp.where(pos < 0, top, back)
                z = jnp.where(me % 2 == 0, zz, nblk - 1 - zz)
                for i in range(ns):
                    out_ref[((k + i) ^ me) * nblk + z] = back[:, i * cap : (i + 1) * cap]
            k += ns


def spread(owner, me, bests, places, counts, zs, nsec, cap):
    nblk = len(zs)
    widest = max(b.shape[1] for b in bests) // nblk
    return pl.pallas_call(
        functools.partial(spread_kernel, len(bests), nblk, counts, zs),
        out_shape=jax.ShapeDtypeStruct((nsec * nblk, 1, cap), F32),
        in_specs=[SMEM, SMEM] + [VMEM] * (len(bests) + nblk),
        out_specs=VMEM,
        scratch_shapes=[pltpu.VMEM((ceil_to(nblk, 8), ceil_to(widest, 128)), F32)],
        compiler_params=pltpu.CompilerParams(vmem_limit_bytes=8 << 20),
        name="spread",
    )(owner, me, *bests, *places)


def pick_kernel(nsec, nblk, pos_ref, got_ref, out_ref, redo_ref):
    count, cap = pos_ref.shape[1], got_ref.shape[2]
    got = jnp.concatenate([got_ref[c * nblk + nblk // 2 - c % 2] for c in range(nsec)], axis=0)
    redo_ref[0] = (jnp.max(got) > 0.5 * REDO).astype(jnp.int32)
    turned = got.T
    total = jnp.zeros((1, count), F32)
    for c in range(nsec):
        hit = lax.broadcasted_iota(jnp.int32, (cap, count), 0) + c * cap == pos_ref[...]
        total = total + jnp.sum(jnp.where(hit, turned[:, c : c + 1], 0.0), axis=0, keepdims=True)
    out_ref[...] = total


def pick(pos, got, nsec, nblk):
    return pl.pallas_call(
        functools.partial(pick_kernel, nsec, nblk),
        out_shape=[
            jax.ShapeDtypeStruct(pos.shape, F32),
            jax.ShapeDtypeStruct((1,), jnp.int32),
        ],
        in_specs=[VMEM, VMEM],
        out_specs=[VMEM, SMEM],
        compiler_params=pltpu.CompilerParams(vmem_limit_bytes=8 << 20),
        name="pick",
    )(pos, got)


def xor(nsec, bits):
    return [(g, g ^ bits) for g in range(nsec)]


def best_of_all(held, owner, me, pos, parts, share, nblk):
    nsec, cap = len(held), held[0].shape[0]
    upper = nblk // 2
    order = sorted((z for z in range(nblk) if z != upper), key=lambda z: abs(z - upper))
    flip = lambda b, core: b if core == 0 else nblk - 1 - b
    routes = [
        [(g * nblk + flip(z, g % 2), g * nblk + flip(upper, g % 2)) for g in range(nsec)]
        for z in order
    ]
    arrays, biases, bests, places = [], [], [], []
    for q, (lo, hi) in enumerate(parts):
        group, place = squeeze(held[lo:hi], share[q] * (hi - lo) * cap // 16)
        places.append(place)
        blocks = [group]
        for route in routes:
            blocks.append(lax.ppermute(group, AXES, route))
        if len(parts) == 1:
            bests = [every(owner, blocks)]
        else:
            new, bias, bests = pair(owner, blocks, arrays, biases, bests, 3)
            arrays.append(new)
            biases.append(bias)
    place = jnp.concatenate(places, axis=1)
    spots = [place]
    for route in routes:
        spots.append(lax.ppermute(place, AXES, route))
    counts = tuple(hi - lo for lo, hi in parts)
    sorted_out = spread(owner, me, bests, spots, counts, (upper, *order), nsec, cap)
    got = lax.all_to_all(sorted_out, AXES, split_axis=0, concat_axis=0, tiled=True)
    return pick(pos, got, nsec, nblk)


def on_device(embed, dest, slot):
    count = embed.shape[0]
    nsec, nblk = lax.axis_size("grp"), lax.axis_size("blk")
    cap = 2 * count // (nsec * nblk) * nblk
    grp, blk = lax.axis_index("grp"), lax.axis_index("blk")
    me = grp.astype(jnp.int32).reshape(1)
    owner = (blk == nblk // 2 - grp % 2).astype(jnp.int32).reshape(1)
    pos, *sent = pack(embed, dest, me, nsec, cap, nblk)
    quarter = nsec // 4
    parts = [(0, quarter), (quarter, 3 * quarter), (3 * quarter, nsec)]
    held = [sent[0]]
    for k in range(1, nsec):
        held.append(lax.ppermute(sent[k], "grp", xor(nsec, k)))
    best, redo = best_of_all(held, owner, me, pos, parts, (12, 11, 12), nblk)
    best = lax.cond(
        redo[0] > 0,
        lambda: best_of_all(held, owner, me, pos, [(0, nsec)], (16,), nblk)[0],
        lambda: best,
    )
    return best.reshape(count)


def solution(mesh):
    placed = (P(AXES, None), P(AXES), P(AXES))
    return jax.shard_map(
        on_device, mesh=mesh, in_specs=placed, out_specs=P(AXES), check_vma=False
    )
```

```python
import functools

import jax
import jax.numpy as jnp
from jax import lax
from jax.experimental import pallas as pl
from jax.experimental.pallas import tpu as pltpu
from jax.sharding import PartitionSpec as P


AXES = ("grp", "blk")
PAD = 2.0
LOW = -8.0
FULL = 4.0
REDO = 100.0
F32 = jnp.float32
BF16 = jnp.bfloat16
VMEM = pl.BlockSpec(memory_space=pltpu.VMEM)
SMEM = pl.BlockSpec(memory_space=pltpu.SMEM)
TILE = 256


def pack_kernel(nsec, cap, stride, nblk, me_ref, dest_hbm, embed_hbm, *refs):
    pos_ref, sections = refs[0], refs[1 : nsec + 1]
    dest_ref, embed_ref, dest_sem, embed_sem = refs[nsec + 1 :]
    dest_copy = pltpu.make_async_copy(dest_hbm, dest_ref, dest_sem)
    embed_copy = pltpu.make_async_copy(embed_hbm, embed_ref, embed_sem)
    dest_copy.start()
    embed_copy.start()
    count = embed_ref.shape[0]
    lower = lax.broadcasted_iota(jnp.int32, (count, count), 0) < lax.broadcasted_iota(
        jnp.int32, (count, count), 1
    )
    lower = lower.astype(F32).astype(BF16)
    dest_copy.wait()
    cluster = lax.div(dest_ref[...], nblk)
    part = cluster ^ me_ref[0]
    onehot = lax.broadcasted_iota(jnp.int32, (nsec, count), 0) == part
    before = jnp.dot(onehot.astype(F32).astype(BF16), lower, preferred_element_type=F32)
    rank = jnp.sum(jnp.where(onehot, before, 0.0), axis=0, keepdims=True).astype(jnp.int32)
    pos_ref[...] = jnp.where(rank < cap, cluster * stride + rank, -1)
    pos = jnp.where(rank < cap, part * cap + rank, -1)
    held = jnp.sum(onehot.astype(F32), axis=1, keepdims=True)
    rows = lax.broadcasted_iota(jnp.int32, (cap, 128), 0).astype(F32)
    first = lax.broadcasted_iota(jnp.int32, (cap, 128), 1) == 0
    embed_copy.wait()
    wide = embed_ref[...].astype(F32)
    unit = (wide * lax.rsqrt(jnp.sum(wide * wide, axis=1, keepdims=True) + 1e-06)).astype(BF16)
    for k, out in enumerate(sections):
        pick = lax.broadcasted_iota(jnp.int32, (cap, count), 0) + k * cap == pos
        value = jnp.dot(pick.astype(F32).astype(BF16), unit, preferred_element_type=F32)
        out[...] = value.astype(BF16)
        many = held[k : k + 1, :]
        head = jnp.where(first & (rows >= many), PAD, value[:, 0:128])
        head = jnp.where(first & (rows == cap - 1.0) & (many > cap), FULL, head)
        out[:, 0:128] = head.astype(BF16)


def pack(embed, dest, me, nsec, cap, stride, nblk):
    count, width = embed.shape
    hbm = pl.BlockSpec(memory_space=pltpu.HBM)
    return pl.pallas_call(
        functools.partial(pack_kernel, nsec, cap, stride, nblk),
        out_shape=[jax.ShapeDtypeStruct((1, count), jnp.int32)]
        + [jax.ShapeDtypeStruct((cap, width), BF16)] * nsec,
        in_specs=[SMEM, hbm, hbm],
        out_specs=[VMEM] * (nsec + 1),
        scratch_shapes=[
            pltpu.VMEM((1, count), jnp.int32),
            pltpu.VMEM((count, width), BF16),
            pltpu.SemaphoreType.DMA,
            pltpu.SemaphoreType.DMA,
        ],
        compiler_params=pltpu.CompilerParams(vmem_limit_bytes=24 << 20),
        name="pack",
    )(me, dest.reshape(1, count), embed)


def scores(left, right):
    return lax.dot_general(left, right, (((1,), (1,)), ((), ())), preferred_element_type=F32)


def first_entries(rows_ref):
    first = lax.broadcasted_iota(jnp.int32, (8, rows_ref.shape[1]), 1) == 0
    return scores(first.astype(F32).astype(BF16), rows_ref[...])[0:1, :]


def squeeze_kernel(nsec, stride, *refs):
    sections, out_ref, pos_ref, all_ref = refs[:nsec], refs[nsec], refs[nsec + 1], refs[nsec + 2]
    room = out_ref.shape[0]
    cap = sections[0].shape[0]
    size = nsec * stride
    for k, section in enumerate(sections):
        all_ref[k * stride : k * stride + cap, :] = section[...]
        if cap < stride:
            all_ref[k * stride + cap : (k + 1) * stride, :] = jnp.full(
                (stride - cap, all_ref.shape[1]), PAD, BF16
            )
    entries = first_entries(all_ref)
    filled = entries < 1.5
    lower = lax.broadcasted_iota(jnp.int32, (size, size), 0) < lax.broadcasted_iota(
        jnp.int32, (size, size), 1
    )
    ones = jnp.broadcast_to(filled.astype(F32), (8, size))
    before = jnp.dot(
        ones.astype(BF16), lower.astype(F32).astype(BF16), preferred_element_type=F32
    )[0:1, :]
    total = jnp.sum(filled.astype(F32), axis=1, keepdims=True)
    left_out = (total > room) | (jnp.max(entries, axis=1, keepdims=True) > 3.0)
    pos = jnp.where(filled, before, -1.0).astype(jnp.int32)
    pos_ref[...] = pos
    pick = (lax.broadcasted_iota(jnp.int32, (room, size), 0) == pos).astype(F32).astype(BF16)
    value = jnp.dot(pick, all_ref[...], preferred_element_type=F32)
    out_ref[...] = value.astype(BF16)
    rows = lax.broadcasted_iota(jnp.int32, (room, 128), 0).astype(F32)
    first = lax.broadcasted_iota(jnp.int32, (room, 128), 1) == 0
    head = jnp.where(first & (rows >= total), PAD, value[:, 0:128])
    head = jnp.where(first & (rows == room - 1.0) & left_out, FULL, head)
    out_ref[:, 0:128] = head.astype(BF16)


def squeeze(sections, room, stride):
    width = sections[0].shape[1]
    size = len(sections) * stride
    return pl.pallas_call(
        functools.partial(squeeze_kernel, len(sections), stride),
        out_shape=[
            jax.ShapeDtypeStruct((room, width), BF16),
            jax.ShapeDtypeStruct((1, size), jnp.int32),
        ],
        in_specs=[VMEM] * len(sections),
        out_specs=[VMEM] * 2,
        scratch_shapes=[pltpu.VMEM((size, width), BF16)],
        compiler_params=pltpu.CompilerParams(vmem_limit_bytes=16 << 20),
        cost_estimate=pl.CostEstimate(
            flops=2 * room * size * width, bytes_accessed=2 * (room + size) * width, transcendentals=0
        ),
        name="squeeze",
    )(*sections)


def bias_of(entries):
    return jnp.where(entries > 3.0, REDO, jnp.where(entries > 1.5, LOW, 0.0))


def pair_kernel(nblk, nold, unroll, owner_ref, *refs):
    refs = list(refs)
    take = lambda n: [refs.pop(0) for _ in range(n)]
    blocks, olds, bias_olds, best_olds = take(nblk), take(nold), take(nold), take(nold)
    (new_ref, bias_ref, best_ref), best_outs = take(3), take(nold)
    (acc_ref,) = take(1)
    rows, size = new_ref.shape[0], blocks[0].shape[0]
    tiles = lambda n: [(lo, min(TILE, n - lo)) for lo in range(0, n, TILE)]

    @pl.when(owner_ref[0] == 1)
    def _():
        for j, block in enumerate(blocks):
            new_ref[j * size : (j + 1) * size, :] = block[...]
        bias_ref[...] = bias_of(first_entries(new_ref))
        down = bias_of(new_ref[:, 0:1].astype(F32))
        acc_ref[...] = jnp.full_like(acc_ref, LOW)

        def fold(start, value):
            part = value[:, 0:128]
            for j in range(1, value.shape[1] // 128):
                part = jnp.maximum(part, value[:, j * 128 : (j + 1) * 128])
            acc_ref[start:, :] = jnp.maximum(acc_ref[start:, :], part)

        col_best = []
        for lo, tile in tiles(rows):
            value = scores(new_ref[lo:, :], new_ref[lo : lo + tile, :])
            same = lax.broadcasted_iota(jnp.int32, (tile, tile), 0) == lax.broadcasted_iota(
                jnp.int32, (tile, tile), 1
            )
            head = jnp.where(same, LOW, value[0:tile])
            value = jnp.concatenate([head, value[tile:]], axis=0) if tile < rows - lo else head
            fold(lo, value + bias_ref[:, lo : lo + tile])
            col_best.append(jnp.max(value + down[lo:, :], axis=0, keepdims=True))
        for old, bias, best, out in zip(olds, bias_olds, best_olds, best_outs):

            def step(i, carry, old=old, bias=bias, best=best, out=out, tile=TILE):
                at = pl.ds(i * TILE, tile) if tile < TILE else pl.ds(pl.multiple_of(i * TILE, TILE), TILE)
                value = scores(new_ref[...], old[at, :])
                fold(0, value + bias[:, at])
                out[:, at] = jnp.maximum(
                    best[:, at], jnp.max(value + down, axis=0, keepdims=True)
                )
                return carry

            full, rest = divmod(old.shape[0], TILE)
            lax.fori_loop(0, full, step, 0, unroll=unroll if full % unroll == 0 else full)
            if rest:
                step(full, 0, tile=rest)
        for j, (lo, tile) in enumerate(tiles(rows)):
            across = jnp.max(acc_ref[lo : lo + tile, :].T, axis=0, keepdims=True)
            best_ref[:, lo : lo + tile] = jnp.maximum(across, col_best[j])


def ceil_to(n, m):
    return -(-n // m) * m


def pair(owner, blocks, olds, biases, bests, unroll):
    nblk, (size, width) = len(blocks), blocks[0].shape
    rows, nold = nblk * size, len(olds)
    row = jax.ShapeDtypeStruct((1, rows), F32)
    flops = 2 * width * rows * (rows // 2 + sum(o.shape[0] for o in olds))
    out = pl.pallas_call(
        functools.partial(pair_kernel, nblk, nold, unroll),
        out_shape=[jax.ShapeDtypeStruct((rows, width), BF16), row, row]
        + [jax.ShapeDtypeStruct(b.shape, F32) for b in bests],
        in_specs=[SMEM] + [VMEM] * (nblk + 3 * nold),
        out_specs=[VMEM] * (3 + nold),
        scratch_shapes=[pltpu.VMEM((rows, 128), F32)],
        compiler_params=pltpu.CompilerParams(vmem_limit_bytes=24 << 20),
        cost_estimate=pl.CostEstimate(
            flops=flops, bytes_accessed=rows * width * 2, transcendentals=0
        ),
        name="pair",
    )(owner, *blocks, *olds, *biases, *bests)
    return out[0], out[1], list(out[3:]) + [out[2]]


def every_kernel(nblk, owner_ref, *refs):
    blocks, best_ref, all_ref = refs[:nblk], refs[nblk], refs[nblk + 1]
    size = blocks[0].shape[0]
    count = nblk * size // TILE

    @pl.when(owner_ref[0] == 1)
    def _():
        for j, block in enumerate(blocks):
            all_ref[j * size : (j + 1) * size, :] = block[...]
        same = lax.broadcasted_iota(jnp.int32, (TILE, TILE), 0) == lax.broadcasted_iota(
            jnp.int32, (TILE, TILE), 1
        )
        span = lambda i: pl.ds(pl.multiple_of(i * TILE, TILE), TILE)

        def column(j, carry):
            def row(i, best):
                rows = all_ref[span(i), :]
                value = scores(rows, all_ref[span(j), :]) + bias_of(rows[:, 0:1].astype(F32))
                value = jnp.where(same & (i == j), LOW, value)
                return jnp.maximum(best, jnp.max(value, axis=0, keepdims=True))

            best_ref[:, span(j)] = lax.fori_loop(0, count, row, jnp.full((1, TILE), LOW, F32))
            return carry

        lax.fori_loop(0, count, column, 0)


def every(owner, blocks):
    nblk, (size, width) = len(blocks), blocks[0].shape
    return pl.pallas_call(
        functools.partial(every_kernel, nblk),
        out_shape=jax.ShapeDtypeStruct((1, nblk * size), F32),
        in_specs=[SMEM] + [VMEM] * nblk,
        out_specs=VMEM,
        scratch_shapes=[pltpu.VMEM((nblk * size, width), BF16)],
        compiler_params=pltpu.CompilerParams(vmem_limit_bytes=28 << 20),
        name="every",
    )(owner, *blocks)


def spread_kernel(nq, nblk, counts, zs, owner_ref, me_ref, *refs):
    bests, places, out_ref, rows_ref = refs[:nq], refs[nq : nq + nblk], refs[-2], refs[-1]
    cap = out_ref.shape[2]

    @pl.when(owner_ref[0] == 1)
    def _():
        me = me_ref[0]
        top = functools.reduce(jnp.maximum, [jnp.max(b[...]) for b in bests])
        k = 0
        for best, ns in zip(bests, counts):
            size = best.shape[1] // nblk
            for j in range(nblk):
                rows_ref[j : j + 1, 0:size] = best[:, j * size : (j + 1) * size]
            turned = rows_ref[...].T
            lo = k * cap
            for j, zz in enumerate(zs):
                pos = places[j][:, lo : lo + ns * cap]
                hit = lax.broadcasted_iota(jnp.int32, (size, ns * cap), 0) == pos
                back = jnp.max(
                    jnp.where(hit, turned[0:size, j : j + 1], LOW), axis=0, keepdims=True
                )
                back = jnp.where(pos < 0, top, back)
                z = jnp.where(me % 2 == 0, zz, nblk - 1 - zz)
                for i in range(ns):
                    out_ref[((k + i) ^ me) * nblk + z] = back[:, i * cap : (i + 1) * cap]
            k += ns


def spread(owner, me, bests, places, counts, zs, nsec, cap):
    nblk = len(zs)
    widest = max(b.shape[1] for b in bests) // nblk
    return pl.pallas_call(
        functools.partial(spread_kernel, len(bests), nblk, counts, zs),
        out_shape=jax.ShapeDtypeStruct((nsec * nblk, 1, cap), F32),
        in_specs=[SMEM, SMEM] + [VMEM] * (len(bests) + nblk),
        out_specs=VMEM,
        scratch_shapes=[pltpu.VMEM((ceil_to(nblk, 8), ceil_to(widest, 128)), F32)],
        compiler_params=pltpu.CompilerParams(vmem_limit_bytes=8 << 20),
        name="spread",
    )(owner, me, *bests, *places)


def pick_kernel(nsec, nblk, pos_ref, got_ref, out_ref, redo_ref):
    count, cap = pos_ref.shape[1], got_ref.shape[2]
    got = jnp.concatenate([got_ref[c * nblk + nblk // 2 - c % 2] for c in range(nsec)], axis=0)
    redo_ref[0] = (jnp.max(got) > 0.5 * REDO).astype(jnp.int32)
    turned = got.T
    total = jnp.zeros((1, count), F32)
    for c in range(nsec):
        hit = lax.broadcasted_iota(jnp.int32, (cap, count), 0) + c * cap == pos_ref[...]
        total = total + jnp.sum(jnp.where(hit, turned[:, c : c + 1], 0.0), axis=0, keepdims=True)
    out_ref[...] = total


def pick(pos, got, nsec, nblk):
    return pl.pallas_call(
        functools.partial(pick_kernel, nsec, nblk),
        out_shape=[
            jax.ShapeDtypeStruct(pos.shape, F32),
            jax.ShapeDtypeStruct((1,), jnp.int32),
        ],
        in_specs=[VMEM, VMEM],
        out_specs=[VMEM, SMEM],
        compiler_params=pltpu.CompilerParams(vmem_limit_bytes=8 << 20),
        name="pick",
    )(pos, got)


def xor(nsec, bits):
    return [(g, g ^ bits) for g in range(nsec)]


def best_of_all(embed, dest, owner, me, cap, stride, parts, rooms, nsec, nblk):
    pos, *sent = pack(embed, dest, me, nsec, cap, stride, nblk)
    held = [sent[0]]
    for k in range(1, nsec):
        held.append(lax.ppermute(sent[k], "grp", xor(nsec, k)))
    upper = nblk // 2
    order = sorted((z for z in range(nblk) if z != upper), key=lambda z: abs(z - upper))
    flip = lambda b, core: b if core == 0 else nblk - 1 - b
    routes = [
        [(g * nblk + flip(z, g % 2), g * nblk + flip(upper, g % 2)) for g in range(nsec)]
        for z in order
    ]
    arrays, biases, bests, places = [], [], [], []
    for q, (lo, hi) in enumerate(parts):
        group, place = squeeze(held[lo:hi], rooms[q], stride)
        places.append(place)
        blocks = [group]
        for route in routes:
            blocks.append(lax.ppermute(group, AXES, route))
        if len(parts) == 1:
            bests = [every(owner, blocks)]
        else:
            new, bias, bests = pair(owner, blocks, arrays, biases, bests, 3)
            arrays.append(new)
            biases.append(bias)
    place = jnp.concatenate(places, axis=1)
    spots = [place]
    for route in routes:
        spots.append(lax.ppermute(place, AXES, route))
    counts = tuple(hi - lo for lo, hi in parts)
    sorted_out = spread(owner, me, bests, spots, counts, (upper, *order), nsec, stride)
    got = lax.all_to_all(sorted_out, AXES, split_axis=0, concat_axis=0, tiled=True)
    return pick(pos, got, nsec, nblk)


def on_device(embed, dest, slot):
    count = embed.shape[0]
    nsec, nblk = lax.axis_size("grp"), lax.axis_size("blk")
    cap = 2 * count // (nsec * nblk) * nblk
    grp, blk = lax.axis_index("grp"), lax.axis_index("blk")
    me = grp.astype(jnp.int32).reshape(1)
    owner = (blk == nblk // 2 - grp % 2).astype(jnp.int32).reshape(1)
    quarter = nsec // 4
    parts = [(0, quarter), (quarter, 3 * quarter), (3 * quarter, nsec)]
    rooms = [3 * quarter * cap // 4, 11 * quarter * cap // 8, 3 * quarter * cap // 4]
    best, redo = best_of_all(embed, dest, owner, me, 7 * cap // 8, cap, parts, rooms, nsec, nblk)
    best = lax.cond(
        redo[0] > 0,
        lambda: best_of_all(
            embed, dest, owner, me, cap, cap, [(0, nsec)], [nsec * cap], nsec, nblk
        )[0],
        lambda: best,
    )
    return best.reshape(count)


def solution(mesh):
    placed = (P(AXES, None), P(AXES), P(AXES))
    return jax.shard_map(
        on_device, mesh=mesh, in_specs=placed, out_specs=P(AXES), check_vma=False
    )
```

```python
import functools

import jax
import jax.numpy as jnp
from jax import lax
from jax.experimental import pallas as pl
from jax.experimental.pallas import tpu as pltpu
from jax.sharding import PartitionSpec as P


AXES = ("grp", "blk")
PAD = 2.0
LOW = -8.0
FULL = 4.0
REDO = 100.0
F32 = jnp.float32
BF16 = jnp.bfloat16
VMEM = pl.BlockSpec(memory_space=pltpu.VMEM)
SMEM = pl.BlockSpec(memory_space=pltpu.SMEM)
TILE = 256


def pack_kernel(nsec, cap, stride, nblk, me_ref, dest_hbm, embed_hbm, *refs):
    pos_ref, place_ref, held_ref, unit_ref, *sections = refs[:-4]
    dest_ref, embed_ref, dest_sem, embed_sem = refs[-4:]
    dest_copy = pltpu.make_async_copy(dest_hbm, dest_ref, dest_sem)
    embed_copy = pltpu.make_async_copy(embed_hbm, embed_ref, embed_sem)
    dest_copy.start()
    embed_copy.start()
    count = embed_ref.shape[0]
    lower = lax.broadcasted_iota(jnp.int32, (count, count), 0) < lax.broadcasted_iota(
        jnp.int32, (count, count), 1
    )
    lower = lower.astype(F32).astype(BF16)
    dest_copy.wait()
    cluster = lax.div(dest_ref[...], nblk)
    part = cluster ^ me_ref[0]
    onehot = lax.broadcasted_iota(jnp.int32, (nsec, count), 0) == part
    before = jnp.dot(onehot.astype(F32).astype(BF16), lower, preferred_element_type=F32)
    rank = jnp.sum(jnp.where(onehot, before, 0.0), axis=0, keepdims=True).astype(jnp.int32)
    pos_ref[...] = jnp.where(rank < cap, cluster * stride + rank, -1)
    pos = jnp.where(rank < cap, part * cap + rank, -1)
    held = jnp.sum(onehot.astype(F32), axis=1, keepdims=True)
    place_ref[...] = pos
    held_ref[...] = held
    embed_copy.wait()
    wide = embed_ref[...].astype(F32)
    unit = (wide * lax.rsqrt(jnp.sum(wide * wide, axis=1, keepdims=True) + 1e-06)).astype(BF16)
    unit_ref[...] = unit
    fill(unit, pos, held, sections, 0, cap)


def fill(unit, pos, held, sections, base, cap):
    rows = lax.broadcasted_iota(jnp.int32, (cap, 128), 0).astype(F32)
    first = lax.broadcasted_iota(jnp.int32, (cap, 128), 1) == 0
    number = len(sections) * cap
    pick = lax.broadcasted_iota(jnp.int32, (number, pos.shape[1]), 0) + base * cap == pos
    packed = jnp.dot(pick.astype(F32).astype(BF16), unit, preferred_element_type=F32)
    for k, out in enumerate(sections):
        value = packed[k * cap : (k + 1) * cap, :]
        out[...] = value.astype(BF16)
        many = held[base + k : base + k + 1, :]
        head = jnp.where(first & (rows >= many), PAD, value[:, 0:128])
        head = jnp.where(first & (rows == cap - 1.0) & (many > cap), FULL, head)
        out[:, 0:128] = head.astype(BF16)


def rest_kernel(base, cap, unit_ref, place_ref, held_ref, *sections):
    fill(unit_ref[...], place_ref[...], held_ref[...], sections, base, cap)


def pack(embed, dest, me, nsec, now, cap, stride, nblk):
    count, width = embed.shape
    hbm = pl.BlockSpec(memory_space=pltpu.HBM)
    section = jax.ShapeDtypeStruct((cap, width), BF16)
    places = jax.ShapeDtypeStruct((1, count), jnp.int32)
    pos, place, held, unit, *sections = pl.pallas_call(
        functools.partial(pack_kernel, nsec, cap, stride, nblk),
        out_shape=[places, places, jax.ShapeDtypeStruct((nsec, 1), F32)]
        + [jax.ShapeDtypeStruct((count, width), BF16)]
        + [section] * now,
        in_specs=[SMEM, hbm, hbm],
        out_specs=[VMEM] * (now + 4),
        scratch_shapes=[
            pltpu.VMEM((1, count), jnp.int32),
            pltpu.VMEM((count, width), BF16),
            pltpu.SemaphoreType.DMA,
            pltpu.SemaphoreType.DMA,
        ],
        compiler_params=pltpu.CompilerParams(vmem_limit_bytes=12 << 20),
        name="pack",
    )(me, dest.reshape(1, count), embed)
    if now < nsec:
        sections += pl.pallas_call(
            functools.partial(rest_kernel, now, cap),
            out_shape=[section] * (nsec - now),
            in_specs=[VMEM] * 3,
            out_specs=[VMEM] * (nsec - now),
            compiler_params=pltpu.CompilerParams(vmem_limit_bytes=8 << 20),
            name="rest",
        )(unit, place, held)
    return pos, sections


def scores(left, right):
    return lax.dot_general(left, right, (((1,), (1,)), ((), ())), preferred_element_type=F32)


def first_entries(rows_ref):
    first = lax.broadcasted_iota(jnp.int32, (8, rows_ref.shape[1]), 1) == 0
    return scores(first.astype(F32).astype(BF16), rows_ref[...])[0:1, :]


def squeeze_kernel(nsec, stride, *refs):
    sections, out_ref, pos_ref, all_ref = refs[:nsec], refs[nsec], refs[nsec + 1], refs[nsec + 2]
    room = out_ref.shape[0]
    cap = sections[0].shape[0]
    size = nsec * stride
    for k, section in enumerate(sections):
        all_ref[k * stride : k * stride + cap, :] = section[...]
        if cap < stride:
            all_ref[k * stride + cap : (k + 1) * stride, :] = jnp.full(
                (stride - cap, all_ref.shape[1]), PAD, BF16
            )
    entries = first_entries(all_ref)
    filled = entries < 1.5
    lower = lax.broadcasted_iota(jnp.int32, (size, size), 0) < lax.broadcasted_iota(
        jnp.int32, (size, size), 1
    )
    ones = jnp.broadcast_to(filled.astype(F32), (8, size))
    before = jnp.dot(
        ones.astype(BF16), lower.astype(F32).astype(BF16), preferred_element_type=F32
    )[0:1, :]
    total = jnp.sum(filled.astype(F32), axis=1, keepdims=True)
    left_out = (total > room) | (jnp.max(entries, axis=1, keepdims=True) > 3.0)
    pos = jnp.where(filled, before, -1.0).astype(jnp.int32)
    pos_ref[...] = pos
    pick = (lax.broadcasted_iota(jnp.int32, (room, size), 0) == pos).astype(F32).astype(BF16)
    value = jnp.dot(pick, all_ref[...], preferred_element_type=F32)
    out_ref[...] = value.astype(BF16)
    rows = lax.broadcasted_iota(jnp.int32, (room, 128), 0).astype(F32)
    first = lax.broadcasted_iota(jnp.int32, (room, 128), 1) == 0
    head = jnp.where(first & (rows >= total), PAD, value[:, 0:128])
    head = jnp.where(first & (rows == room - 1.0) & left_out, FULL, head)
    out_ref[:, 0:128] = head.astype(BF16)


def squeeze(sections, room, stride):
    width = sections[0].shape[1]
    size = len(sections) * stride
    return pl.pallas_call(
        functools.partial(squeeze_kernel, len(sections), stride),
        out_shape=[
            jax.ShapeDtypeStruct((room, width), BF16),
            jax.ShapeDtypeStruct((1, size), jnp.int32),
        ],
        in_specs=[VMEM] * len(sections),
        out_specs=[VMEM] * 2,
        scratch_shapes=[pltpu.VMEM((size, width), BF16)],
        compiler_params=pltpu.CompilerParams(vmem_limit_bytes=16 << 20),
        cost_estimate=pl.CostEstimate(
            flops=2 * room * size * width, bytes_accessed=2 * (room + size) * width, transcendentals=0
        ),
        name="squeeze",
    )(*sections)


def bias_of(entries):
    return jnp.where(entries > 3.0, REDO, jnp.where(entries > 1.5, LOW, 0.0))


def pair_kernel(nblk, nold, last, unroll, owner_ref, *refs):
    refs = list(refs)
    take = lambda n: [refs.pop(0) for _ in range(n)]
    blocks, olds, bias_olds, best_olds = take(nblk), take(nold), take(nold), take(nold)
    if last:
        (best_ref, *best_outs), (new_ref, bias_ref, acc_ref) = take(1 + nold), take(3)
    else:
        (best_ref, *best_outs), (new_ref, bias_ref), (acc_ref,) = take(1 + nold), take(2), take(1)
    rows, size = new_ref.shape[0], blocks[0].shape[0]
    tiles = lambda n: [(lo, min(TILE, n - lo)) for lo in range(0, n, TILE)]

    @pl.when(owner_ref[0] == 1)
    def _():
        for j, block in enumerate(blocks):
            new_ref[j * size : (j + 1) * size, :] = block[...]
        bias_ref[...] = bias_of(first_entries(new_ref))
        down = bias_of(new_ref[:, 0:1].astype(F32))
        acc_ref[...] = jnp.full_like(acc_ref, LOW)

        def fold(start, value):
            part = value[:, 0:128]
            for j in range(1, value.shape[1] // 128):
                part = jnp.maximum(part, value[:, j * 128 : (j + 1) * 128])
            acc_ref[start:, :] = jnp.maximum(acc_ref[start:, :], part)

        col_best = []
        for lo, tile in tiles(rows):
            value = scores(new_ref[lo:, :], new_ref[lo : lo + tile, :])
            same = lax.broadcasted_iota(jnp.int32, (tile, tile), 0) == lax.broadcasted_iota(
                jnp.int32, (tile, tile), 1
            )
            head = jnp.where(same, LOW, value[0:tile])
            value = jnp.concatenate([head, value[tile:]], axis=0) if tile < rows - lo else head
            fold(lo, value + bias_ref[:, lo : lo + tile])
            col_best.append(jnp.max(value + down[lo:, :], axis=0, keepdims=True))
        for old, bias, best, out in zip(olds, bias_olds, best_olds, best_outs):

            def step(i, carry, old=old, bias=bias, best=best, out=out, tile=TILE):
                at = pl.ds(i * TILE, tile) if tile < TILE else pl.ds(pl.multiple_of(i * TILE, TILE), TILE)
                value = scores(new_ref[...], old[at, :])
                fold(0, value + bias[:, at])
                out[:, at] = jnp.maximum(
                    best[:, at], jnp.max(value + down, axis=0, keepdims=True)
                )
                return carry

            full, rest = divmod(old.shape[0], TILE)
            lax.fori_loop(0, full, step, 0, unroll=unroll if full % unroll == 0 else full)
            if rest:
                step(full, 0, tile=rest)
        for j, (lo, tile) in enumerate(tiles(rows)):
            across = jnp.max(acc_ref[lo : lo + tile, :].T, axis=0, keepdims=True)
            best_ref[:, lo : lo + tile] = jnp.maximum(across, col_best[j])


def ceil_to(n, m):
    return -(-n // m) * m


def pair(owner, blocks, olds, biases, bests, last, unroll):
    nblk, (size, width) = len(blocks), blocks[0].shape
    rows, nold = nblk * size, len(olds)
    row = jax.ShapeDtypeStruct((1, rows), F32)
    flops = 2 * width * rows * (rows // 2 + sum(o.shape[0] for o in olds))
    kept = [] if last else [jax.ShapeDtypeStruct((rows, width), BF16), row]
    scratch = [pltpu.VMEM((rows, width), BF16), pltpu.VMEM((1, rows), F32)] if last else []
    out = pl.pallas_call(
        functools.partial(pair_kernel, nblk, nold, last, unroll),
        out_shape=[row] + [jax.ShapeDtypeStruct(b.shape, F32) for b in bests] + kept,
        in_specs=[SMEM] + [VMEM] * (nblk + 3 * nold),
        out_specs=[VMEM] * (1 + nold + len(kept)),
        scratch_shapes=scratch + [pltpu.VMEM((rows, 128), F32)],
        compiler_params=pltpu.CompilerParams(vmem_limit_bytes=24 << 20),
        cost_estimate=pl.CostEstimate(
            flops=flops, bytes_accessed=rows * width * 2, transcendentals=0
        ),
        name="pair",
    )(owner, *blocks, *olds, *biases, *bests)
    return list(out[1 : 1 + nold]) + [out[0]], out[1 + nold :]


def every_kernel(nblk, owner_ref, *refs):
    blocks, best_ref, all_ref = refs[:nblk], refs[nblk], refs[nblk + 1]
    size = blocks[0].shape[0]
    count = nblk * size // TILE

    @pl.when(owner_ref[0] == 1)
    def _():
        for j, block in enumerate(blocks):
            all_ref[j * size : (j + 1) * size, :] = block[...]
        same = lax.broadcasted_iota(jnp.int32, (TILE, TILE), 0) == lax.broadcasted_iota(
            jnp.int32, (TILE, TILE), 1
        )
        span = lambda i: pl.ds(pl.multiple_of(i * TILE, TILE), TILE)

        def column(j, carry):
            def row(i, best):
                rows = all_ref[span(i), :]
                value = scores(rows, all_ref[span(j), :]) + bias_of(rows[:, 0:1].astype(F32))
                value = jnp.where(same & (i == j), LOW, value)
                return jnp.maximum(best, jnp.max(value, axis=0, keepdims=True))

            best_ref[:, span(j)] = lax.fori_loop(0, count, row, jnp.full((1, TILE), LOW, F32))
            return carry

        lax.fori_loop(0, count, column, 0)


def every(owner, blocks):
    nblk, (size, width) = len(blocks), blocks[0].shape
    return pl.pallas_call(
        functools.partial(every_kernel, nblk),
        out_shape=jax.ShapeDtypeStruct((1, nblk * size), F32),
        in_specs=[SMEM] + [VMEM] * nblk,
        out_specs=VMEM,
        scratch_shapes=[pltpu.VMEM((nblk * size, width), BF16)],
        compiler_params=pltpu.CompilerParams(vmem_limit_bytes=28 << 20),
        name="every",
    )(owner, *blocks)


def spread_kernel(nq, nblk, counts, zs, owner_ref, me_ref, *refs):
    bests, places, out_ref, rows_ref = refs[:nq], refs[nq : nq + nblk], refs[-2], refs[-1]
    cap = out_ref.shape[2]

    @pl.when(owner_ref[0] == 1)
    def _():
        me = me_ref[0]
        top = functools.reduce(jnp.maximum, [jnp.max(b[...]) for b in bests])
        k = 0
        for best, ns in zip(bests, counts):
            size = best.shape[1] // nblk
            for j in range(nblk):
                rows_ref[j : j + 1, 0:size] = best[:, j * size : (j + 1) * size]
            turned = rows_ref[...].T
            lo = k * cap
            for j, zz in enumerate(zs):
                pos = places[j][:, lo : lo + ns * cap]
                hit = lax.broadcasted_iota(jnp.int32, (size, ns * cap), 0) == pos
                back = jnp.max(
                    jnp.where(hit, turned[0:size, j : j + 1], LOW), axis=0, keepdims=True
                )
                back = jnp.where(pos < 0, top, back)
                z = jnp.where(me % 2 == 0, zz, nblk - 1 - zz)
                for i in range(ns):
                    out_ref[((k + i) ^ me) * nblk + z] = back[:, i * cap : (i + 1) * cap]
            k += ns


def spread(owner, me, bests, places, counts, zs, nsec, cap):
    nblk = len(zs)
    widest = max(b.shape[1] for b in bests) // nblk
    return pl.pallas_call(
        functools.partial(spread_kernel, len(bests), nblk, counts, zs),
        out_shape=jax.ShapeDtypeStruct((nsec * nblk, 1, cap), F32),
        in_specs=[SMEM, SMEM] + [VMEM] * (len(bests) + nblk),
        out_specs=VMEM,
        scratch_shapes=[pltpu.VMEM((ceil_to(nblk, 8), ceil_to(widest, 128)), F32)],
        compiler_params=pltpu.CompilerParams(vmem_limit_bytes=8 << 20),
        name="spread",
    )(owner, me, *bests, *places)


def pick_kernel(nsec, nblk, pos_ref, got_ref, out_ref, redo_ref):
    count, cap = pos_ref.shape[1], got_ref.shape[2]
    got = jnp.concatenate([got_ref[c * nblk + nblk // 2 - c % 2] for c in range(nsec)], axis=0)
    redo_ref[0] = (jnp.max(got) > 0.5 * REDO).astype(jnp.int32)
    turned = got.T
    total = jnp.zeros((1, count), F32)
    for c in range(nsec):
        hit = lax.broadcasted_iota(jnp.int32, (cap, count), 0) + c * cap == pos_ref[...]
        total = total + jnp.sum(jnp.where(hit, turned[:, c : c + 1], 0.0), axis=0, keepdims=True)
    out_ref[...] = total


def pick(pos, got, nsec, nblk):
    return pl.pallas_call(
        functools.partial(pick_kernel, nsec, nblk),
        out_shape=[
            jax.ShapeDtypeStruct(pos.shape, F32),
            jax.ShapeDtypeStruct((1,), jnp.int32),
        ],
        in_specs=[VMEM, VMEM],
        out_specs=[VMEM, SMEM],
        compiler_params=pltpu.CompilerParams(vmem_limit_bytes=8 << 20),
        name="pick",
    )(pos, got)


def xor(nsec, bits):
    return [(g, g ^ bits) for g in range(nsec)]


def best_of_all(embed, dest, owner, me, cap, stride, parts, rooms, nsec, nblk):
    pos, sent = pack(embed, dest, me, nsec, parts[-1][0] or nsec, cap, stride, nblk)
    held = [sent[0]]
    for k in range(1, nsec):
        held.append(lax.ppermute(sent[k], "grp", xor(nsec, k)))
    upper = nblk // 2
    order = sorted((z for z in range(nblk) if z != upper), key=lambda z: abs(z - upper))
    flip = lambda b, core: b if core == 0 else nblk - 1 - b
    routes = [
        [(g * nblk + flip(z, g % 2), g * nblk + flip(upper, g % 2)) for g in range(nsec)]
        for z in order
    ]
    arrays, biases, bests, places = [], [], [], []
    for q, (lo, hi) in enumerate(parts):
        group, place = squeeze(held[lo:hi], rooms[q], stride)
        places.append(place)
        blocks = [group]
        for route in routes:
            blocks.append(lax.ppermute(group, AXES, route))
        if len(parts) == 1:
            bests = [every(owner, blocks)]
        else:
            last = q == len(parts) - 1
            bests, kept = pair(owner, blocks, arrays, biases, bests, last, 3)
            arrays.extend(kept[:1])
            biases.extend(kept[1:])
    place = jnp.concatenate(places, axis=1)
    spots = [place]
    for route in routes:
        spots.append(lax.ppermute(place, AXES, route))
    counts = tuple(hi - lo for lo, hi in parts)
    sorted_out = spread(owner, me, bests, spots, counts, (upper, *order), nsec, stride)
    got = lax.all_to_all(sorted_out, AXES, split_axis=0, concat_axis=0, tiled=True)
    return pick(pos, got, nsec, nblk)


def on_device(embed, dest, slot):
    count = embed.shape[0]
    nsec, nblk = lax.axis_size("grp"), lax.axis_size("blk")
    cap = 2 * count // (nsec * nblk) * nblk
    grp, blk = lax.axis_index("grp"), lax.axis_index("blk")
    me = grp.astype(jnp.int32).reshape(1)
    owner = (blk == nblk // 2 - grp % 2).astype(jnp.int32).reshape(1)
    quarter = nsec // 4
    parts = [(0, quarter), (quarter, 3 * quarter), (3 * quarter, nsec)]
    rooms = [3 * quarter * cap // 4, 11 * quarter * cap // 8, 3 * quarter * cap // 4]
    best, redo = best_of_all(embed, dest, owner, me, 7 * cap // 8, cap, parts, rooms, nsec, nblk)
    best = lax.cond(
        redo[0] > 0,
        lambda: best_of_all(
            embed, dest, owner, me, cap, cap, [(0, nsec)], [nsec * cap], nsec, nblk
        )[0],
        lambda: best,
    )
    return best.reshape(count)


def solution(mesh):
    placed = (P(AXES, None), P(AXES), P(AXES))
    return jax.shard_map(
        on_device, mesh=mesh, in_specs=placed, out_specs=P(AXES), check_vma=False
    )
```

```python
import functools

import jax
import jax.numpy as jnp
from jax import lax
from jax.experimental import pallas as pl
from jax.experimental.pallas import tpu as pltpu
from jax.sharding import PartitionSpec as P


AXES = ("grp", "blk")
PAD = 2.0
LOW = -8.0
FULL = 4.0
REDO = 100.0
F32 = jnp.float32
BF16 = jnp.bfloat16
VMEM = pl.BlockSpec(memory_space=pltpu.VMEM)
SMEM = pl.BlockSpec(memory_space=pltpu.SMEM)
TILE = 256


def pack_kernel(nsec, cap, stride, nblk, me_ref, dest_hbm, embed_hbm, *refs):
    pos_ref, place_ref, held_ref, unit_ref, *sections = refs[:-4]
    dest_ref, embed_ref, dest_sem, embed_sem = refs[-4:]
    dest_copy = pltpu.make_async_copy(dest_hbm, dest_ref, dest_sem)
    embed_copy = pltpu.make_async_copy(embed_hbm, embed_ref, embed_sem)
    dest_copy.start()
    embed_copy.start()
    count = embed_ref.shape[0]
    lower = lax.broadcasted_iota(jnp.int32, (count, count), 0) < lax.broadcasted_iota(
        jnp.int32, (count, count), 1
    )
    lower = lower.astype(F32).astype(BF16)
    dest_copy.wait()
    cluster = lax.div(dest_ref[...], nblk)
    part = cluster ^ me_ref[0]
    onehot = lax.broadcasted_iota(jnp.int32, (nsec, count), 0) == part
    before = jnp.dot(onehot.astype(F32).astype(BF16), lower, preferred_element_type=F32)
    rank = jnp.sum(jnp.where(onehot, before, 0.0), axis=0, keepdims=True).astype(jnp.int32)
    pos_ref[...] = jnp.where(rank < cap, cluster * stride + rank, -1)
    pos = jnp.where(rank < cap, part * cap + rank, -1)
    held = jnp.sum(onehot.astype(F32), axis=1, keepdims=True)
    place_ref[...] = pos
    held_ref[...] = held
    embed_copy.wait()
    wide = embed_ref[...].astype(F32)
    unit = (wide * lax.rsqrt(jnp.sum(wide * wide, axis=1, keepdims=True) + 1e-06)).astype(BF16)
    unit_ref[...] = unit
    fill(unit, pos, held, sections, 0, cap)


def fill(unit, pos, held, sections, base, cap):
    rows = lax.broadcasted_iota(jnp.int32, (cap, 128), 0).astype(F32)
    first = lax.broadcasted_iota(jnp.int32, (cap, 128), 1) == 0
    number = len(sections) * cap
    pick = lax.broadcasted_iota(jnp.int32, (number, pos.shape[1]), 0) + base * cap == pos
    packed = jnp.dot(pick.astype(F32).astype(BF16), unit, preferred_element_type=F32)
    for k, out in enumerate(sections):
        value = packed[k * cap : (k + 1) * cap, :]
        out[...] = value.astype(BF16)
        many = held[base + k : base + k + 1, :]
        head = jnp.where(first & (rows >= many), PAD, value[:, 0:128])
        head = jnp.where(first & (rows == cap - 1.0) & (many > cap), FULL, head)
        out[:, 0:128] = head.astype(BF16)


def rest_kernel(base, cap, unit_ref, place_ref, held_ref, *sections):
    fill(unit_ref[...], place_ref[...], held_ref[...], sections, base, cap)


def pack(embed, dest, me, nsec, now, cap, stride, nblk):
    count, width = embed.shape
    hbm = pl.BlockSpec(memory_space=pltpu.HBM)
    section = jax.ShapeDtypeStruct((cap, width), BF16)
    places = jax.ShapeDtypeStruct((1, count), jnp.int32)
    pos, place, held, unit, *sections = pl.pallas_call(
        functools.partial(pack_kernel, nsec, cap, stride, nblk),
        out_shape=[places, places, jax.ShapeDtypeStruct((nsec, 1), F32)]
        + [jax.ShapeDtypeStruct((count, width), BF16)]
        + [section] * now,
        in_specs=[SMEM, hbm, hbm],
        out_specs=[VMEM] * (now + 4),
        scratch_shapes=[
            pltpu.VMEM((1, count), jnp.int32),
            pltpu.VMEM((count, width), BF16),
            pltpu.SemaphoreType.DMA,
            pltpu.SemaphoreType.DMA,
        ],
        compiler_params=pltpu.CompilerParams(vmem_limit_bytes=12 << 20),
        name="pack",
    )(me, dest.reshape(1, count), embed)
    if now < nsec:
        sections += pl.pallas_call(
            functools.partial(rest_kernel, now, cap),
            out_shape=[section] * (nsec - now),
            in_specs=[VMEM] * 3,
            out_specs=[VMEM] * (nsec - now),
            compiler_params=pltpu.CompilerParams(vmem_limit_bytes=8 << 20),
            name="rest",
        )(unit, place, held)
    return pos, sections


def scores(left, right):
    return lax.dot_general(left, right, (((1,), (1,)), ((), ())), preferred_element_type=F32)


def first_entries(rows_ref):
    first = lax.broadcasted_iota(jnp.int32, (8, rows_ref.shape[1]), 1) == 0
    return scores(first.astype(F32).astype(BF16), rows_ref[...])[0:1, :]


def squeeze_kernel(nsec, stride, *refs):
    sections, out_ref, pos_ref, all_ref = refs[:nsec], refs[nsec], refs[nsec + 1], refs[nsec + 2]
    room = out_ref.shape[0]
    cap = sections[0].shape[0]
    size = nsec * stride
    for k, section in enumerate(sections):
        all_ref[k * stride : k * stride + cap, :] = section[...]
        if cap < stride:
            all_ref[k * stride + cap : (k + 1) * stride, :] = jnp.full(
                (stride - cap, all_ref.shape[1]), PAD, BF16
            )
    entries = first_entries(all_ref)
    filled = entries < 1.5
    lower = lax.broadcasted_iota(jnp.int32, (size, size), 0) < lax.broadcasted_iota(
        jnp.int32, (size, size), 1
    )
    ones = jnp.broadcast_to(filled.astype(F32), (8, size))
    before = jnp.dot(
        ones.astype(BF16), lower.astype(F32).astype(BF16), preferred_element_type=F32
    )[0:1, :]
    total = jnp.sum(filled.astype(F32), axis=1, keepdims=True)
    left_out = (total > room) | (jnp.max(entries, axis=1, keepdims=True) > 3.0)
    pos = jnp.where(filled, before, -1.0).astype(jnp.int32)
    pos_ref[...] = pos
    pick = (lax.broadcasted_iota(jnp.int32, (room, size), 0) == pos).astype(F32).astype(BF16)
    value = jnp.dot(pick, all_ref[...], preferred_element_type=F32)
    out_ref[...] = value.astype(BF16)
    rows = lax.broadcasted_iota(jnp.int32, (room, 128), 0).astype(F32)
    first = lax.broadcasted_iota(jnp.int32, (room, 128), 1) == 0
    head = jnp.where(first & (rows >= total), PAD, value[:, 0:128])
    head = jnp.where(first & (rows == room - 1.0) & left_out, FULL, head)
    out_ref[:, 0:128] = head.astype(BF16)


def squeeze(sections, room, stride):
    width = sections[0].shape[1]
    size = len(sections) * stride
    return pl.pallas_call(
        functools.partial(squeeze_kernel, len(sections), stride),
        out_shape=[
            jax.ShapeDtypeStruct((room, width), BF16),
            jax.ShapeDtypeStruct((1, size), jnp.int32),
        ],
        in_specs=[VMEM] * len(sections),
        out_specs=[VMEM] * 2,
        scratch_shapes=[pltpu.VMEM((size, width), BF16)],
        compiler_params=pltpu.CompilerParams(vmem_limit_bytes=16 << 20),
        cost_estimate=pl.CostEstimate(
            flops=2 * room * size * width, bytes_accessed=2 * (room + size) * width, transcendentals=0
        ),
        name="squeeze",
    )(*sections)


def bias_of(entries):
    return jnp.where(entries > 3.0, REDO, jnp.where(entries > 1.5, LOW, 0.0))


def pair_kernel(nblk, nold, last, unroll, owner_ref, *refs):
    refs = list(refs)
    take = lambda n: [refs.pop(0) for _ in range(n)]
    blocks, olds, bias_olds, best_olds = take(nblk), take(nold), take(nold), take(nold)
    if last:
        (best_ref, *best_outs), (new_ref, bias_ref, acc_ref) = take(1 + nold), take(3)
    else:
        (best_ref, *best_outs), (new_ref, bias_ref), (acc_ref,) = take(1 + nold), take(2), take(1)
    rows = new_ref.shape[0]
    tiles = lambda n: [(lo, min(TILE, n - lo)) for lo in range(0, n, TILE)]

    @pl.when(owner_ref[0] == 1)
    def _():
        at = 0
        for block in blocks:
            new_ref[at : at + block.shape[0], :] = block[...]
            at += block.shape[0]
        bias_ref[...] = bias_of(first_entries(new_ref))
        down = bias_of(new_ref[:, 0:1].astype(F32))
        acc_ref[...] = jnp.full_like(acc_ref, LOW)

        def fold(start, value):
            part = value[:, 0:128]
            for j in range(1, value.shape[1] // 128):
                part = jnp.maximum(part, value[:, j * 128 : (j + 1) * 128])
            acc_ref[start:, 0 : part.shape[1]] = jnp.maximum(
                acc_ref[start:, 0 : part.shape[1]], part
            )
            rest = value.shape[1] % 128
            if rest and value.shape[1] > 128:
                acc_ref[start:, 0:rest] = jnp.maximum(acc_ref[start:, 0:rest], value[:, -rest:])

        col_best = []
        for lo, tile in tiles(rows):
            value = scores(new_ref[lo:, :], new_ref[lo : lo + tile, :])
            same = lax.broadcasted_iota(jnp.int32, (tile, tile), 0) == lax.broadcasted_iota(
                jnp.int32, (tile, tile), 1
            )
            head = jnp.where(same, LOW, value[0:tile])
            value = jnp.concatenate([head, value[tile:]], axis=0) if tile < rows - lo else head
            fold(lo, value + bias_ref[:, lo : lo + tile])
            col_best.append(jnp.max(value + down[lo:, :], axis=0, keepdims=True))
        for old, bias, best, out in zip(olds, bias_olds, best_olds, best_outs):

            def step(i, carry, old=old, bias=bias, best=best, out=out, tile=TILE):
                at = pl.ds(i * TILE, tile) if tile < TILE else pl.ds(pl.multiple_of(i * TILE, TILE), TILE)
                value = scores(new_ref[...], old[at, :])
                fold(0, value + bias[:, at])
                out[:, at] = jnp.maximum(
                    best[:, at], jnp.max(value + down, axis=0, keepdims=True)
                )
                return carry

            full, rest = divmod(old.shape[0], TILE)
            lax.fori_loop(0, full, step, 0, unroll=unroll if full % unroll == 0 else full)
            if rest:
                step(full, 0, tile=rest)
        for j, (lo, tile) in enumerate(tiles(rows)):
            across = jnp.max(acc_ref[lo : lo + tile, :].T, axis=0, keepdims=True)
            best_ref[:, lo : lo + tile] = jnp.maximum(across, col_best[j])


def ceil_to(n, m):
    return -(-n // m) * m


def pair(owner, blocks, olds, biases, bests, last, unroll):
    nblk, width = len(blocks), blocks[0].shape[1]
    rows, nold = sum(b.shape[0] for b in blocks), len(olds)
    row = jax.ShapeDtypeStruct((1, rows), F32)
    flops = 2 * width * rows * (rows // 2 + sum(o.shape[0] for o in olds))
    kept = [] if last else [jax.ShapeDtypeStruct((rows, width), BF16), row]
    scratch = [pltpu.VMEM((rows, width), BF16), pltpu.VMEM((1, rows), F32)] if last else []
    out = pl.pallas_call(
        functools.partial(pair_kernel, nblk, nold, last, unroll),
        out_shape=[row] + [jax.ShapeDtypeStruct(b.shape, F32) for b in bests] + kept,
        in_specs=[SMEM] + [VMEM] * (nblk + 3 * nold),
        out_specs=[VMEM] * (1 + nold + len(kept)),
        scratch_shapes=scratch + [pltpu.VMEM((rows, 128), F32)],
        compiler_params=pltpu.CompilerParams(vmem_limit_bytes=24 << 20),
        cost_estimate=pl.CostEstimate(
            flops=flops, bytes_accessed=rows * width * 2, transcendentals=0
        ),
        name="pair",
    )(owner, *blocks, *olds, *biases, *bests)
    return list(out[1 : 1 + nold]) + [out[0]], out[1 + nold :]


def every_kernel(nblk, owner_ref, *refs):
    blocks, best_ref, all_ref = refs[:nblk], refs[nblk], refs[nblk + 1]
    size = blocks[0].shape[0]
    count = nblk * size // TILE

    @pl.when(owner_ref[0] == 1)
    def _():
        for j, block in enumerate(blocks):
            all_ref[j * size : (j + 1) * size, :] = block[...]
        same = lax.broadcasted_iota(jnp.int32, (TILE, TILE), 0) == lax.broadcasted_iota(
            jnp.int32, (TILE, TILE), 1
        )
        span = lambda i: pl.ds(pl.multiple_of(i * TILE, TILE), TILE)

        def column(j, carry):
            def row(i, best):
                rows = all_ref[span(i), :]
                value = scores(rows, all_ref[span(j), :]) + bias_of(rows[:, 0:1].astype(F32))
                value = jnp.where(same & (i == j), LOW, value)
                return jnp.maximum(best, jnp.max(value, axis=0, keepdims=True))

            best_ref[:, span(j)] = lax.fori_loop(0, count, row, jnp.full((1, TILE), LOW, F32))
            return carry

        lax.fori_loop(0, count, column, 0)


def every(owner, blocks):
    nblk, (size, width) = len(blocks), blocks[0].shape
    return pl.pallas_call(
        functools.partial(every_kernel, nblk),
        out_shape=jax.ShapeDtypeStruct((1, nblk * size), F32),
        in_specs=[SMEM] + [VMEM] * nblk,
        out_specs=VMEM,
        scratch_shapes=[pltpu.VMEM((nblk * size, width), BF16)],
        compiler_params=pltpu.CompilerParams(vmem_limit_bytes=28 << 20),
        name="every",
    )(owner, *blocks)


def spread_kernel(nset, nblk, counts, where, zs, owner_ref, me_ref, *refs):
    bests, places, out_ref, rows_ref = refs[:nset], refs[nset : nset + nblk], refs[-2], refs[-1]
    cap = out_ref.shape[2]

    @pl.when(owner_ref[0] == 1)
    def _():
        me = me_ref[0]
        top = functools.reduce(jnp.maximum, [jnp.max(b[...]) for b in bests])
        k = 0
        for q, ns in enumerate(counts):
            for j in range(nblk):
                which, lo, size = where[q][j]
                rows_ref[j : j + 1, 0:size] = bests[which][:, lo : lo + size]
            turned = rows_ref[...].T
            lo = k * cap
            for j, zz in enumerate(zs):
                pos = places[j][:, lo : lo + ns * cap]
                hit = lax.broadcasted_iota(jnp.int32, (size, ns * cap), 0) == pos
                back = jnp.max(
                    jnp.where(hit, turned[0:size, j : j + 1], LOW), axis=0, keepdims=True
                )
                back = jnp.where(pos < 0, top, back)
                z = jnp.where(me % 2 == 0, zz, nblk - 1 - zz)
                for i in range(ns):
                    out_ref[((k + i) ^ me) * nblk + z] = back[:, i * cap : (i + 1) * cap]
            k += ns


def spread(owner, me, bests, places, counts, where, zs, nsec, cap):
    nblk = len(zs)
    widest = max(size for row in where for _, _, size in row)
    return pl.pallas_call(
        functools.partial(spread_kernel, len(bests), nblk, counts, where, zs),
        out_shape=jax.ShapeDtypeStruct((nsec * nblk, 1, cap), F32),
        in_specs=[SMEM, SMEM] + [VMEM] * (len(bests) + nblk),
        out_specs=VMEM,
        scratch_shapes=[pltpu.VMEM((ceil_to(nblk, 8), ceil_to(widest, 128)), F32)],
        compiler_params=pltpu.CompilerParams(vmem_limit_bytes=8 << 20),
        name="spread",
    )(owner, me, *bests, *places)


def pick_kernel(nsec, nblk, pos_ref, got_ref, out_ref, redo_ref):
    count, cap = pos_ref.shape[1], got_ref.shape[2]
    got = jnp.concatenate([got_ref[c * nblk + nblk // 2 - c % 2] for c in range(nsec)], axis=0)
    redo_ref[0] = (jnp.max(got) > 0.5 * REDO).astype(jnp.int32)
    turned = got.T
    total = jnp.zeros((1, count), F32)
    for c in range(nsec):
        hit = lax.broadcasted_iota(jnp.int32, (cap, count), 0) + c * cap == pos_ref[...]
        total = total + jnp.sum(jnp.where(hit, turned[:, c : c + 1], 0.0), axis=0, keepdims=True)
    out_ref[...] = total


def pick(pos, got, nsec, nblk):
    return pl.pallas_call(
        functools.partial(pick_kernel, nsec, nblk),
        out_shape=[
            jax.ShapeDtypeStruct(pos.shape, F32),
            jax.ShapeDtypeStruct((1,), jnp.int32),
        ],
        in_specs=[VMEM, VMEM],
        out_specs=[VMEM, SMEM],
        compiler_params=pltpu.CompilerParams(vmem_limit_bytes=8 << 20),
        name="pick",
    )(pos, got)


def xor(nsec, bits):
    return [(g, g ^ bits) for g in range(nsec)]


def best_of_all(embed, dest, owner, me, cap, stride, parts, rooms, nsec, nblk):
    pos, sent = pack(embed, dest, me, nsec, parts[-1][0] or nsec, cap, stride, nblk)
    held = [sent[0]]
    for k in range(1, nsec):
        held.append(lax.ppermute(sent[k], "grp", xor(nsec, k)))
    upper = nblk // 2
    order = sorted((z for z in range(nblk) if z != upper), key=lambda z: abs(z - upper))
    flip = lambda b, core: b if core == 0 else nblk - 1 - b
    routes = [
        [(g * nblk + flip(z, g % 2), g * nblk + flip(upper, g % 2)) for g in range(nsec)]
        for z in order
    ]
    places, sets, where = [], [[] for _ in parts], []
    for q, (lo, hi) in enumerate(parts):
        group, place = squeeze(held[lo:hi], rooms[q], stride)
        places.append(place)
        where.append([])
        for j in range(nblk):
            which = max(q - 1, 0) if j == 0 else q
            block = group
            if j:
                block = lax.ppermute(group, AXES, routes[j - 1])
            where[q].append((which, sum(b.shape[0] for b in sets[which]), group.shape[0]))
            sets[which].append(block)
    arrays, biases, bests = [], [], []
    if len(parts) == 1:
        bests = [every(owner, sets[0])]
    else:
        for q, blocks in enumerate(sets):
            last = q == len(parts) - 1
            bests, kept = pair(owner, blocks, arrays, biases, bests, last, 3)
            arrays.extend(kept[:1])
            biases.extend(kept[1:])
    place = jnp.concatenate(places, axis=1)
    spots = [place]
    for route in routes:
        spots.append(lax.ppermute(place, AXES, route))
    counts = tuple(hi - lo for lo, hi in parts)
    sorted_out = spread(
        owner, me, bests, spots, counts, where, (upper, *order), nsec, stride
    )
    got = lax.all_to_all(sorted_out, AXES, split_axis=0, concat_axis=0, tiled=True)
    return pick(pos, got, nsec, nblk)


def on_device(embed, dest, slot):
    count = embed.shape[0]
    nsec, nblk = lax.axis_size("grp"), lax.axis_size("blk")
    cap = 2 * count // (nsec * nblk) * nblk
    grp, blk = lax.axis_index("grp"), lax.axis_index("blk")
    me = grp.astype(jnp.int32).reshape(1)
    owner = (blk == nblk // 2 - grp % 2).astype(jnp.int32).reshape(1)
    quarter = nsec // 4
    parts = [(0, quarter), (quarter, 3 * quarter), (3 * quarter, nsec)]
    rooms = [3 * quarter * cap // 4, 21 * quarter * cap // 16, 3 * quarter * cap // 4]
    best, redo = best_of_all(embed, dest, owner, me, 7 * cap // 8, cap, parts, rooms, nsec, nblk)
    best = lax.cond(
        redo[0] > 0,
        lambda: best_of_all(
            embed, dest, owner, me, cap, cap, [(0, nsec)], [nsec * cap], nsec, nblk
        )[0],
        lambda: best,
    )
    return best.reshape(count)


def solution(mesh):
    placed = (P(AXES, None), P(AXES), P(AXES))
    return jax.shard_map(
        on_device, mesh=mesh, in_specs=placed, out_specs=P(AXES), check_vma=False
    )
```
